256 devices in a mesh: blk: 64 (over y_lo, z, x), rep: 4 (over y_hi, core).
Axes of the slice: x: 4, y: 4 (y_hi: 2, y_lo: 2; y = y_hi * 2 + y_lo), z: 8, core: 2. Of those that a mesh axis runs over, the one named last changes fastest.
Arguments:
- points: bfloat16 [49152, 1024], P('blk'), may hold values from -6 to 6
- w_in: bfloat16 [1024, 512], replicated, may hold values from -0.1875 to 0.1875
- b_in: float32 [512], replicated, may hold values from -3 to 3
- w_out: bfloat16 [512, 64], replicated, may hold values from -0.25 to 0.25
- inv_scale: float32 [64], replicated, may hold values from 0.05 to 0.5
- solves: bfloat16 [64, 49152], P(None, 'blk'), may hold values from -1 to 1
- probes: bfloat16 [64, 49152], P(None, 'blk'), may hold values from -1 to 1
Outputs:
- feat_grad: float32 [64, 49152], P(None, ('blk', 'rep'))
- grad_w_in: float32 [1024, 512], replicated
- grad_b_in: float32 [512], replicated
- grad_w_out: float32 [512, 64], replicated
The draws below stay inside these ranges and needn't reach their ends.
All inputs are finite; a program needn't handle non-finite values.
Results may differ from the reference program's by a relative error of at most 0.034.
Values may be sent and summed in bfloat16 or wider, within the bound.
A program may use at most 64 MiB of HBM per device.

```python
import math
import jax
import jax.numpy as jnp
from jax import lax

DIN = 1024
HID = 512
FEAT = 64
PAIRS = 64
TOK_DEV = 768
NPTS = 49152
N_REP = 4


def block_scale(rng, dims, shards, least, largest):
    def one(axis_at, shards_of):
        steps = jax.random.uniform(jax.random.fold_in(jax.random.fold_in(rng, 6), axis_at), (shards_of,), jnp.float32, least / len(shards), largest / len(shards))
        return jnp.repeat(jnp.exp(steps), dims[axis_at] // shards_of).reshape((-1,) + (1,) * (len(dims) - axis_at - 1))

    loudness = one(*shards[0])
    for cut in shards[1:]:
        loudness = loudness * one(*cut)
    return loudness


def normal_values(stream_key, shape, deviation, limit, shards=(), dtype=jnp.bfloat16):
    level = block_scale(stream_key, shape, shards, -0.22, 0.18) if shards else 1.0
    array = jax.random.normal(stream_key, shape, jnp.float32) * deviation * level
    return jnp.minimum(jnp.maximum(array, -limit), limit).astype(dtype)


def setup_inputs(seed: int = 0) -> dict:
    key_of = jax.random.split(jax.random.key(seed), 8)
    points = normal_values(key_of[0], (NPTS, DIN), 1.0, 6.0, ((0, 64),))
    w_in = normal_values(key_of[1], (DIN, HID), DIN ** -0.5, 0.1875)
    b_in = normal_values(key_of[2], (HID,), 0.5, 3.0, (), jnp.float32)
    w_out = normal_values(key_of[3], (HID, FEAT), HID ** -0.5, 0.25)
    inv_scale = jnp.clip(jnp.exp(jax.random.uniform(key_of[4], (FEAT,), jnp.float32, math.log(0.05), math.log(0.5))), 0.05, 0.5)
    solves = normal_values(key_of[5], (PAIRS, NPTS), (2.5 / NPTS ** 0.25), 1.0, ((1, 64),))
    probes = normal_values(key_of[6], (PAIRS, NPTS), (2.5 / NPTS ** 0.25), 1.0, ((1, 64),))
    return {"points": points, "w_in": w_in, "b_in": b_in, "w_out": w_out, "inv_scale": inv_scale, "solves": solves, "probes": probes}


def couple(own_y, own_pair, own_sq, visitor, feat):
    vis_y = visitor[:feat]
    vis_pair = visitor[feat:]
    vis_sq = lax.optimization_barrier(jnp.sum(jnp.square(vis_y.astype(jnp.float32)), axis=0))
    cross = lax.dot_general(own_y, vis_y, (((0,), (0,)), ((), ())), preferred_element_type=jnp.float32)
    kernel = jnp.exp(-0.5 * (own_sq[:, None] + vis_sq[None, :] - 2.0 * cross))
    coupling = lax.dot_general(own_pair, vis_pair, (((0,), (0,)), ((), ())), preferred_element_type=jnp.float32)
    weight_b = (coupling * kernel).astype(jnp.bfloat16)
    totals = lax.optimization_barrier(jnp.sum(weight_b.astype(jnp.float32), axis=1))
    pull = lax.dot_general(vis_y, weight_b, (((1,), (1,)), ((), ())), preferred_element_type=jnp.float32)
    return (totals, pull)

def reference(points, w_in, b_in, w_out, inv_scale, solves, probes):
    hidden = jnp.tanh(jnp.dot(points, w_in, preferred_element_type=jnp.float32) + b_in).astype(jnp.bfloat16)
    pre = lax.dot_general(w_out, hidden, (((0,), (1,)), ((), ())), preferred_element_type=jnp.float32)
    scaled = (pre * inv_scale[:, None]).astype(jnp.bfloat16)
    sq = lax.optimization_barrier(jnp.sum(jnp.square(scaled.astype(jnp.float32)), axis=0))
    own_pair = jnp.concatenate([solves, probes], axis=0)
    visitor = jnp.concatenate([scaled, probes, solves], axis=0)
    blocks = NPTS // TOK_DEV
    width = TOK_DEV * N_REP
    cols = NPTS // width
    rows_y = scaled.reshape(FEAT, blocks, TOK_DEV).transpose(1, 0, 2)
    rows_pair = own_pair.reshape(2 * PAIRS, blocks, TOK_DEV).transpose(1, 0, 2)
    rows_sq = sq.reshape(blocks, TOK_DEV)
    col_vis = visitor.reshape(FEAT + 2 * PAIRS, cols, width).transpose(1, 0, 2)

    def one_row(item):
        own_y, pair_rows, sq_rows = item

        def step(carry, vis):
            totals, pull = couple(own_y, pair_rows, sq_rows, vis, FEAT)
            return ((carry[0] + totals, carry[1] + pull), None)
        init = (jnp.zeros((TOK_DEV,), jnp.float32), jnp.zeros((FEAT, TOK_DEV), jnp.float32))
        result, unused = lax.scan(step, init, col_vis)
        return result
    totals, pull = lax.map(one_row, (rows_y, rows_pair, rows_sq))
    totals = totals.reshape(NPTS)
    pull = pull.transpose(1, 0, 2).reshape(FEAT, NPTS)
    feat_grad = (pull - scaled.astype(jnp.float32) * totals[None, :]) * inv_scale[:, None]
    grad_b16 = feat_grad.astype(jnp.bfloat16)
    back = lax.dot_general(grad_b16, w_out, (((0,), (1,)), ((), ())), preferred_element_type=jnp.float32)
    hid32 = hidden.astype(jnp.float32)
    pre_grad = back * (1.0 - hid32 * hid32)
    norm = 1.0 / jnp.sqrt(jnp.float32(NPTS))
    grad_w_in = lax.dot_general(points, pre_grad.astype(jnp.bfloat16), (((0,), (0,)), ((), ())), preferred_element_type=jnp.float32) * norm
    grad_b_in = lax.optimization_barrier(jnp.sum(pre_grad, axis=0)) * norm
    grad_w_out = lax.dot_general(hidden, grad_b16, (((0,), (1,)), ((), ())), preferred_element_type=jnp.float32) * norm
    return (feat_grad, grad_w_in, grad_b_in, grad_w_out)
```

```python
import math

import jax
import jax.numpy as jnp
from jax import lax
from jax.experimental import pallas as pl
from jax.experimental.pallas import tpu as pltpu
from jax.sharding import PartitionSpec as P

MESH = pl.DeviceIdType.MESH
F32 = jnp.float32
BF16 = jnp.bfloat16
DIN, HID, FEAT, TOK, QUARTER = 1024, 512, 64, 768, 192
NX, NZ = 4, 8
ROWS = 144
NPTS = 49152


def dot(a, b, ca, cb):
    return lax.dot_general(a, b, (((ca,), (cb,)), ((), ())), preferred_element_type=F32)


def place():
    blk = lax.axis_index("blk")
    rep = lax.axis_index("rep")
    x = lax.rem(blk, NX)
    z = lax.rem(lax.div(blk, NX), NZ)
    y_lo = lax.div(blk, NX * NZ)
    return x, z, y_lo, lax.div(rep, 2), lax.rem(rep, 2)


def device(x, z, y_lo, y_hi, c):
    return ((y_lo * NZ + z) * NX + x, y_hi * 2 + c)


def greet(peers):
    barrier = pltpu.get_barrier_semaphore()
    for peer in peers:
        pl.semaphore_signal(barrier, inc=1, device_id=peer, device_id_type=MESH)
    pl.semaphore_wait(barrier, len(peers))


def grads_kernel(points, hidden, grad, w_out, out, msg, recv_a, stage_b, recv_b, chunk, send_sem, recv_sem):
    x, z, y_lo, y_hi, c = place()
    rep = y_hi * 2 + c
    cell = y_lo * NX + x
    plane = []
    column = []
    for d in range(1, 8):
        other = lax.rem(cell + d, 8)
        plane.append((lax.rem(other, NX), lax.div(other, NX)))
        column.append(lax.rem(z + d, NZ))
    greet(
        [device(px, z, py, y_hi, c) for px, py in plane]
        + [device(x, pz, y_lo, y_hi, c) for pz in column]
        + [device(x, z, y_lo, 1 - y_hi, c), device(x, z, y_lo, y_hi, 1 - c)]
    )

    def copy(at, src, dst, peer):
        return pltpu.make_async_remote_copy(
            src_ref=src,
            dst_ref=dst,
            send_sem=send_sem.at[at],
            recv_sem=recv_sem.at[at],
            device_id=peer,
            device_id_type=MESH,
        )

    norm = 1.0 / math.sqrt(NPTS)
    g = grad[...]
    h32 = hidden[...].astype(F32)
    pre = dot(g, w_out[...], 0, 1) * (1.0 - h32 * h32)
    bias = jnp.sum(pre, axis=0, keepdims=True) * norm
    slab = points[:, pl.ds(pl.multiple_of(rep * 256, 256), 256)]
    gw = dot(slab, pre.astype(BF16), 0, 0) * norm
    gwo = dot(grad[pl.ds(pl.multiple_of(rep * 16, 16), 16), :], hidden[...], 1, 0) * norm
    msg[0, 0:128, :] = gw[0:128].astype(BF16)
    msg[1, 0:128, :] = gw[128:256].astype(BF16)
    msg[0, 128:144, :] = gwo.astype(BF16)
    msg[1, 128:144, :] = jnp.broadcast_to(bias, (16, HID)).astype(BF16)

    def lanes(px):
        return pl.ds(pl.multiple_of(px * 128, 128), 128)

    copies = []
    for d in range(1, 8):
        px, py = plane[d - 1]
        copies.append(copy(d - 1, msg.at[py, :, lanes(px)], recv_a.at[d - 1], device(px, z, py, y_hi, c)))
        copies[-1].start()
    total = msg[y_lo, :, lanes(x)].astype(F32)
    for d in range(1, 8):
        copies[d - 1].wait_recv()
        total = total + recv_a[d - 1].astype(F32)
    total_b = total.astype(BF16)
    for b in range(NZ):
        stage_b[b, 0:16, :] = total_b[b * 16 : b * 16 + 16]
        stage_b[b, 16:32, :] = total_b[128:144]
    for d in range(1, 8):
        pz = column[d - 1]
        copies.append(copy(6 + d, stage_b.at[pz], recv_b.at[d - 1], device(x, pz, y_lo, y_hi, c)))
        copies[-1].start()
    tile = stage_b[z].astype(F32)
    for d in range(1, 8):
        copies[6 + d].wait_recv()
        tile = tile + recv_b[d - 1].astype(F32)
    tile_b = tile.astype(BF16)
    mine = pl.ds(pl.multiple_of(z * 16, 16), 16)
    chunk[mine, :] = tile_b[0:16]
    chunk[128:144, :] = tile_b[16:32]
    for d in range(1, 8):
        pz = column[d - 1]
        copies.append(copy(13 + d, chunk.at[mine], chunk.at[mine], device(x, pz, y_lo, y_hi, c)))
        copies[-1].start()
    for d in range(1, 8):
        copies[13 + d].wait_recv()
    out[y_hi, c, y_lo, :, lanes(x)] = chunk[...]
    place_mine = out.at[y_hi, c, y_lo, :, lanes(x)]
    copies.append(copy(21, chunk, place_mine, device(x, z, y_lo, 1 - y_hi, c)))
    copies[21].start()
    copies[21].wait_recv()
    pair = out.at[:, c, y_lo, :, lanes(x)]
    for d in range(1, 8):
        px, py = plane[d - 1]
        copies.append(copy(21 + d, pair, pair, device(px, z, py, y_hi, c)))
        copies[-1].start()
    for d in range(1, 8):
        copies[21 + d].wait_recv()
    half = out.at[:, c]
    copies.append(copy(29, half, half, device(x, z, y_lo, y_hi, 1 - c)))
    copies[29].start()
    copies[29].wait_recv()
    for one in copies:
        one.wait_send()


def grads(points, hidden, grad, w_out):
    vmem = pl.BlockSpec(memory_space=pltpu.VMEM)
    return pl.pallas_call(
        grads_kernel,
        out_shape=jax.ShapeDtypeStruct((2, 2, 2, ROWS, HID), BF16),
        in_specs=[vmem] * 4,
        out_specs=vmem,
        scratch_shapes=[
            pltpu.VMEM((2, ROWS, HID), BF16),
            pltpu.VMEM((7, ROWS, 128), BF16),
            pltpu.VMEM((NZ, 32, 128), BF16),
            pltpu.VMEM((7, 32, 128), BF16),
            pltpu.VMEM((ROWS, 128), BF16),
            pltpu.SemaphoreType.DMA((30,)),
            pltpu.SemaphoreType.DMA((30,)),
        ],
        compiler_params=pltpu.CompilerParams(
            collective_id=1, has_side_effects=True, vmem_limit_bytes=40 << 20
        ),
        name="grads",
    )(points, hidden, grad, w_out)


def unpack(table):
    parts = table.reshape(4, 2, ROWS, HID)
    grad_w_in = parts[:, :, :128, :].reshape(DIN, HID).astype(F32)
    grad_b_in = parts[0, 1, 128, :].astype(F32)
    grad_w_out = parts[:, 0, 128:, :].reshape(FEAT, HID).T.astype(F32)
    return grad_w_in, grad_b_in, grad_w_out


def shifted(block, axis, distance):
    devices = range(lax.axis_size(axis))
    route = [((i - distance) % len(devices), i) for i in devices]
    return lax.ppermute(block, axis, route)


def cut_along(value, dim, count):
    lengths = value.shape
    blocks = value.reshape(*lengths[:dim], count, lengths[dim] // count, *lengths[dim + 1 :])
    return jnp.moveaxis(blocks, dim, 0)


def sum_at_owner(value, axis, dim):
    count = lax.axis_size(axis)
    blocks = lax.all_to_all(cut_along(value, dim, count), axis, 0, 0, tiled=True)
    return jnp.sum(blocks, axis=0)


def couple(own_y, own_pair, own_sq, visitor, feat):
    vis_y = visitor[:feat]
    vis_pair = visitor[feat:]
    vis_sq = jnp.sum(jnp.square(vis_y.astype(jnp.float32)), axis=0)
    cross = lax.dot_general(
        own_y, vis_y, (((0,), (0,)), ((), ())), preferred_element_type=jnp.float32
    )
    kernel = jnp.exp(-0.5 * (own_sq[:, None] + vis_sq[None, :] - 2.0 * cross))
    coupling = lax.dot_general(
        own_pair, vis_pair, (((0,), (0,)), ((), ())), preferred_element_type=jnp.float32
    )
    weight_b = (coupling * kernel).astype(jnp.bfloat16)
    totals = jnp.sum(weight_b.astype(jnp.float32), axis=1)
    pull = lax.dot_general(
        vis_y, weight_b, (((1,), (1,)), ((), ())), preferred_element_type=jnp.float32
    )
    return (totals, pull)


def on_device(points, w_in, b_in, w_out, inv_scale, solves, probes):
    feat = w_out.shape[1]
    reps = lax.axis_size("rep")
    blocks = lax.axis_size("blk")
    rep_index = lax.axis_index("rep")
    rows = points.shape[0]
    levels = reps.bit_length() - 1
    hidden = jnp.tanh(jnp.dot(points, w_in, preferred_element_type=jnp.float32) + b_in).astype(
        jnp.bfloat16
    )
    pre = lax.dot_general(
        w_out, hidden, (((0,), (1,)), ((), ())), preferred_element_type=jnp.float32
    )
    hidden, scaled = (hidden, (pre * inv_scale[:, None]).astype(jnp.bfloat16))
    own_pair = jnp.concatenate([solves, probes], axis=0)
    own_sq = jnp.sum(jnp.square(scaled.astype(jnp.float32)), axis=0)
    scaled32 = scaled.astype(jnp.float32)
    visitor = jnp.concatenate([scaled, probes, solves], axis=0)
    for bit in range(levels):
        moved = shifted(visitor, "blk", -(1 << bit))
        visitor = jnp.where(rep_index // (1 << bit) % 2 == 1, moved, visitor)

    def accumulate(state, vis):
        totals, pull = couple(scaled, own_pair, own_sq, vis, feat)
        return (state[0] + totals, state[1] + pull)

    init = (jnp.zeros((rows,), jnp.float32), jnp.zeros((feat, rows), jnp.float32))
    steps = blocks // reps
    behind = shifted(visitor, "blk", reps)

    def advance_both(index, carry):
        state, ahead_vis, behind_vis = carry
        state = accumulate(accumulate(state, ahead_vis), behind_vis)
        ahead_vis = shifted(ahead_vis, "blk", -reps)
        behind_vis = shifted(behind_vis, "blk", reps)
        return (state, ahead_vis, behind_vis)

    state, ahead_vis, behind_vis = lax.fori_loop(
        0, steps // 2 - 1, advance_both, (init, visitor, behind)
    )
    state = accumulate(accumulate(state, ahead_vis), behind_vis)
    totals, pull = state
    drift = pull - scaled32 * totals[None, :]
    summed = sum_at_owner(drift, "rep", 1)
    feat_grad = summed * inv_scale[:, None]
    grad_b16 = feat_grad.astype(jnp.bfloat16)
    whole = lax.all_gather(grad_b16, "rep", axis=1, tiled=True)
    return (feat_grad, *unpack(grads(points, hidden, whole, w_out)))


def solution(mesh):
    in_specs = (P("blk", None), P(), P(), P(), P(), P(None, "blk"), P(None, "blk"))
    out_specs = (P(None, ("blk", "rep")), P(), P(), P())
    return jax.shard_map(
        on_device, mesh=mesh, in_specs=in_specs, out_specs=out_specs, check_vma=False
    )
```

```python
import math

import jax
import jax.numpy as jnp
from jax import lax
from jax.experimental import pallas as pl
from jax.experimental.pallas import tpu as pltpu
from jax.sharding import PartitionSpec as P

MESH = pl.DeviceIdType.MESH
F32 = jnp.float32
BF16 = jnp.bfloat16
DIN, HID, FEAT, TOK, QUARTER = 1024, 512, 64, 768, 192
HALF = TOK // 2
NX, NZ = 4, 8
ROWS = 144
MSG = 192
AUG = 80
NPTS = 49152


def dot(a, b, ca, cb):
    return lax.dot_general(a, b, (((ca,), (cb,)), ((), ())), preferred_element_type=F32)


def place():
    blk = lax.axis_index("blk")
    rep = lax.axis_index("rep")
    x = lax.rem(blk, NX)
    z = lax.rem(lax.div(blk, NX), NZ)
    y_lo = lax.div(blk, NX * NZ)
    return x, z, y_lo, lax.div(rep, 2), lax.rem(rep, 2)


def device(x, z, y_lo, y_hi, c):
    return ((y_lo * NZ + z) * NX + x, y_hi * 2 + c)


def aligned(start, size, step):
    return pl.ds(pl.multiple_of(start, step), size)


def norm_rows(y, ones_first):
    y32 = y.astype(F32)
    half_sq = -0.5 * jnp.sum(y32 * y32, axis=0, keepdims=True)
    high = half_sq.astype(BF16).astype(F32)
    mid = (half_sq - high).astype(BF16).astype(F32)
    low = (half_sq - high - mid).astype(BF16).astype(F32)
    row = lax.broadcasted_iota(jnp.int32, (16, y.shape[1]), 0)
    base = 3 if ones_first else 0
    ones = 0 if ones_first else 3
    rows = jnp.where((row >= ones) & (row < ones + 3), 1.0, 0.0)
    rows = jnp.where(row == base, high, rows)
    rows = jnp.where(row == base + 1, mid, rows)
    rows = jnp.where(row == base + 2, low, rows)
    return rows.astype(BF16)


def kernel(
    points_in, w_in, b_in, w_out, scale, solves, probes,
    feat_out, out,
    points, hidden, own, vis, left, vis_b, vis_y, vis_q, acc, drift, drift_in,
    quart, quart_in, grads, grad, msg, recv_a, stage_b, recv_b, chunk,
    load_sem, send_sem, recv_sem,
):
    x, z, y_lo, y_hi, c = place()
    rep = y_hi * 2 + c
    step = 1 - 2 * c
    cell = y_lo * NX + x
    here = (x, z, y_lo, y_hi, c)
    plane = []
    column = []
    reps = []
    for d in range(1, 8):
        other = lax.rem(cell + d, 8)
        plane.append((lax.rem(other, NX), lax.div(other, NX)))
        column.append(lax.rem(z + d, NZ))
    for d in range(1, 4):
        other = lax.rem(rep + d, 4)
        reps.append((other, device(x, z, y_lo, lax.div(other, 2), lax.rem(other, 2))))
    peers = (
        [device(px, z, py, y_hi, c) for px, py in plane]
        + [device(x, pz, y_lo, y_hi, c) for pz in column]
        + [peer for _, peer in reps]
    )
    x_next = lax.rem(x + step + NX, NX)
    x_prev = lax.rem(x - step + NX, NX)
    x_far = lax.rem(x + 2, NX)
    next_x = device(x_next, z, y_lo, y_hi, c)
    next_z = device(x, lax.rem(z + step + NZ, NZ), y_lo, y_hi, c)
    next_y = device(x, z, 1 - y_lo, y_hi, c)
    twin = device(x, z, y_lo, y_hi, 1 - c)

    def lanes(index):
        return aligned(index * TOK, TOK, TOK)

    def copy(at, src, dst, peer):
        return pltpu.make_async_remote_copy(
            src_ref=src,
            dst_ref=dst,
            send_sem=send_sem.at[at],
            recv_sem=recv_sem.at[at],
            device_id=peer,
            device_id_type=MESH,
        )

    def load(at, src, dst):
        return pltpu.make_async_copy(src, dst, load_sem.at[at])

    loads = [
        load(0, solves, own.at[FEAT : 2 * FEAT, lanes(x)]),
        load(1, probes, own.at[2 * FEAT : MSG, lanes(x)]),
    ]
    base_loads = [
        load(6, solves, vis.at[0, FEAT : 2 * FEAT]),
        load(7, probes, vis.at[0, 2 * FEAT : MSG]),
    ]
    for i in range(4):
        part = slice(i * QUARTER, (i + 1) * QUARTER)
        loads.append(load(2 + i, points_in.at[part], points.at[part]))
    for one in loads:
        one.start()

    @pl.when(y_hi == 0)
    def _():
        for one in base_loads:
            one.start()

    barrier = pltpu.get_barrier_semaphore()
    for peer in peers:
        pl.semaphore_signal(barrier, inc=1, device_id=peer, device_id_type=MESH)
    pl.semaphore_wait(barrier, len(peers))

    pairs = slice(FEAT, MSG)
    feats = slice(0, FEAT)
    kinds = ((0, pairs), (1, feats))

    def to_x(kind):
        at, rows = kinds[kind]
        part = own.at[rows, lanes(x)]
        return copy(at, part, part, next_x)

    def to_x_far(kind):
        size = FEAT if kind == 0 else FEAT // 2
        first = FEAT + c * FEAT if kind == 0 else c * (FEAT // 2)
        part = own.at[aligned(first, size, size), lanes(x_prev)]
        return copy(2 + kind, part, part, next_x)

    def to_twin(kind):
        at, rows = kinds[kind]
        part = own.at[rows, lanes(x_prev)]
        return copy(4 + at, part, part, twin)

    def to_twin_far(kind):
        size = FEAT if kind == 0 else FEAT // 2
        first = FEAT + c * FEAT if kind == 0 else c * (FEAT // 2)
        part = own.at[aligned(first, size, size), lanes(x_far)]
        return copy(6 + kind, part, part, twin)

    def to_y(kind):
        at, rows = kinds[kind]
        return copy(8 + at, own.at[rows, lanes(x)], vis.at[0, rows], next_y)

    def to_z(kind, hop):
        rows = kinds[kind][1]
        return copy(10 + 4 * kind + hop, vis.at[hop, rows], vis.at[hop + 1, rows], next_z)

    def to_z_last(kind):
        rows = kinds[kind][1]
        half = aligned(c * HALF, HALF, HALF)
        return copy(13 + 4 * kind, vis.at[3, rows, half], vis.at[4, rows, half], next_z)

    loads[0].wait()
    loads[1].wait()
    to_x(0).start()

    @pl.when(y_hi == 0)
    def _():
        for one in base_loads:
            one.wait()
        to_z(0, 0).start()

    @pl.when(y_hi == 1)
    def _():
        to_y(0).start()

    for i in range(4):
        part = slice(i * QUARTER, (i + 1) * QUARTER)
        loads[2 + i].wait()
        pre = dot(points[part], w_in[...], 1, 0) + b_in[...]
        hidden[part] = jnp.tanh(pre).astype(BF16)
    scaled = (dot(w_out[...], hidden[...], 0, 1) * scale[...]).astype(BF16)
    own[0:FEAT, lanes(x)] = scaled

    to_x(1).start()

    @pl.when(y_hi == 0)
    def _():
        vis[0, 0:FEAT, :] = scaled
        to_z(1, 0).start()

    @pl.when(y_hi == 1)
    def _():
        to_y(1).start()

    to_x(0).wait_recv()
    to_x_far(0).start()
    to_twin(0).start()

    def ready(index):
        y = own[0:FEAT, lanes(index)]
        left[0:FEAT, lanes(index)] = y
        left[FEAT:AUG, lanes(index)] = norm_rows(y, False)
        left[AUG:128, lanes(index)] = jnp.zeros((128 - AUG, TOK), BF16)

    def derive(slot, first, size):
        at = aligned(first, size, HALF)
        y = vis[slot, 0:FEAT, at]
        augmented = jnp.concatenate([y, norm_rows(y, True)], axis=0)
        vis_b[:, 0:size] = augmented
        padded = jnp.concatenate([augmented, jnp.zeros((128 - AUG, size), BF16)], axis=0)
        vis_y[0:size, :] = padded.T
        swapped = jnp.concatenate([vis[slot, 2 * FEAT : MSG, at], vis[slot, FEAT : 2 * FEAT, at]], axis=0)
        vis_q[0:size, :] = swapped.T

    def couple(i, size):
        exponent = dot(vis_y[0:size, :], left[:, i], 1, 0)
        coupling = dot(vis_q[0:size, :], own[FEAT:MSG, i], 1, 0)
        weight = (coupling * jnp.exp(exponent)).astype(BF16)
        return dot(vis_b[:, 0:size], weight, 1, 0)

    ready(x)

    @pl.when(y_hi == 1)
    def _():
        to_y(0).wait_recv()
        to_z(0, 0).start()
        to_y(1).wait_recv()
        to_z(1, 0).start()

    derive(0, c * HALF, HALF)
    acc[:, lanes(x)] = couple(lanes(x), HALF)
    to_x(1).wait_recv()
    to_x_far(1).start()
    to_twin(1).start()
    to_x_far(0).wait_recv()
    to_twin_far(0).start()
    to_x_far(1).wait_recv()
    to_twin_far(1).start()
    ready(x_prev)
    to_twin(0).wait_recv()
    to_twin(1).wait_recv()
    ready(x_next)
    to_twin_far(0).wait_recv()
    to_twin_far(1).wait_recv()
    ready(x_far)

    def first_tiles(k, carry):
        i = lanes(lax.rem(x + k, NX))
        acc[:, i] = couple(i, HALF)
        return carry

    lax.fori_loop(1, NX, first_tiles, 0)

    def visit(hop, carry):
        to_z(0, hop - 1).wait_recv()
        to_z(1, hop - 1).wait_recv()

        @pl.when(hop < 3)
        def _():
            to_z(0, hop).start()
            to_z(1, hop).start()

        @pl.when(hop == 3)
        def _():
            to_z_last(0).start()
            to_z_last(1).start()

        derive(hop, 0, TOK)

        def tiles(k, inner):
            i = aligned(k * 2 * TOK, 2 * TOK, 2 * TOK)
            acc[:, i] += couple(i, TOK)
            return inner

        return lax.fori_loop(0, 2, tiles, carry)

    lax.fori_loop(1, 4, visit, 0)
    to_z_last(0).wait_recv()
    to_z_last(1).wait_recv()
    derive(4, c * HALF, HALF)

    drifts = []

    def finish(index):
        i = lanes(index)
        pull = acc[:, i] + couple(i, HALF)
        return pull[0:FEAT] - own[0:FEAT, i].astype(F32) * pull[FEAT : FEAT + 1]

    for k in (2, 1, 3):
        index = lax.rem(x + k, NX)
        drift[k - 1] = finish(index).astype(BF16)
        drifts.append(copy(17 + k, drift.at[k - 1], drift_in.at[k - 1], device(index, z, y_lo, y_hi, c)))
        drifts[-1].start()
    total = finish(x)
    for one in drifts:
        one.wait_recv()
    for k in range(3):
        total = total + drift_in[k].astype(F32)
    for q in range(4):
        quart[q] = total[:, q * QUARTER : (q + 1) * QUARTER]
    quarters = []
    for d in range(1, 4):
        other, peer = reps[d - 1]
        quarters.append(copy(20 + d, quart.at[other], quart_in.at[d - 1], peer))
        quarters[-1].start()
    mine = quart[rep]
    for d in range(3):
        quarters[d].wait_recv()
        mine = mine + quart_in[d]
    mine = mine * scale[...]
    feat_out[...] = mine
    grads[rep] = mine.astype(BF16)
    gathers = []
    for d in range(1, 4):
        gathers.append(copy(23 + d, grads.at[rep], grads.at[rep], reps[d - 1][1]))
        gathers[-1].start()
    for one in gathers:
        one.wait_recv()
    for q in range(4):
        grad[:, q * QUARTER : (q + 1) * QUARTER] = grads[q]

    norm = 1.0 / math.sqrt(NPTS)
    h32 = hidden[...].astype(F32)
    pre = dot(grad[...], w_out[...], 0, 1) * (1.0 - h32 * h32)
    bias = jnp.sum(pre, axis=0, keepdims=True) * norm
    slab = points[:, aligned(rep * 256, 256, 256)]
    gw = dot(slab, pre.astype(BF16), 0, 0) * norm
    gwo = dot(grad[aligned(rep * 16, 16, 16), :], hidden[...], 1, 0) * norm
    msg[0, 0:128, :] = gw[0:128].astype(BF16)
    msg[1, 0:128, :] = gw[128:256].astype(BF16)
    msg[0, 128:144, :] = gwo.astype(BF16)
    msg[1, 128:144, :] = jnp.broadcast_to(bias, (16, HID)).astype(BF16)

    def strip(px):
        return aligned(px * 128, 128, 128)

    copies = []
    for d in range(1, 8):
        px, py = plane[d - 1]
        copies.append(copy(26 + d, msg.at[py, :, strip(px)], recv_a.at[d - 1], device(px, z, py, y_hi, c)))
        copies[-1].start()
    summed = msg[y_lo, :, strip(x)].astype(F32)
    for d in range(1, 8):
        copies[d - 1].wait_recv()
        summed = summed + recv_a[d - 1].astype(F32)
    summed_b = summed.astype(BF16)
    for b in range(NZ):
        stage_b[b, 0:16, :] = summed_b[b * 16 : b * 16 + 16]
        stage_b[b, 16:32, :] = summed_b[128:144]
    for d in range(1, 8):
        pz = column[d - 1]
        copies.append(copy(33 + d, stage_b.at[pz], recv_b.at[d - 1], device(x, pz, y_lo, y_hi, c)))
        copies[-1].start()
    tile = stage_b[z].astype(F32)
    for d in range(1, 8):
        copies[6 + d].wait_recv()
        tile = tile + recv_b[d - 1].astype(F32)
    tile_b = tile.astype(BF16)
    band = aligned(z * 16, 16, 16)
    chunk[band, :] = tile_b[0:16]
    chunk[128:144, :] = tile_b[16:32]
    for d in range(1, 8):
        pz = column[d - 1]
        copies.append(copy(40 + d, chunk.at[band], chunk.at[band], device(x, pz, y_lo, y_hi, c)))
        copies[-1].start()
    for d in range(1, 8):
        copies[13 + d].wait_recv()
    out[y_hi, c, y_lo, :, strip(x)] = chunk[...]
    mate = copy(48, chunk, out.at[y_hi, c, y_lo, :, strip(x)], device(x, z, y_lo, 1 - y_hi, c))
    mate.start()
    mate.wait_recv()
    copies.append(mate)
    pair = out.at[:, c, y_lo, :, strip(x)]
    spread = []
    for d in range(1, 8):
        px, py = plane[d - 1]
        spread.append(copy(48 + d, pair, pair, device(px, z, py, y_hi, c)))
        spread[-1].start()
    for one in spread:
        one.wait_recv()
    half = out.at[:, c]
    last = copy(56, half, half, twin)
    last.start()
    last.wait_recv()
    for one in drifts + quarters + gathers + copies + spread + [last]:
        one.wait_send()
    for kind in range(2):
        to_x(kind).wait_send()
        to_x_far(kind).wait_send()
        to_twin(kind).wait_send()
        to_twin_far(kind).wait_send()
        for hop in range(3):
            to_z(kind, hop).wait_send()
        to_z_last(kind).wait_send()

        @pl.when(y_hi == 1)
        def _():
            to_y(kind).wait_send()


def on_device(points, w_in, b_in, w_out, inv_scale, solves, probes):
    vmem = pl.BlockSpec(memory_space=pltpu.VMEM)
    hbm = pl.BlockSpec(memory_space=pl.ANY)
    feat_grad, table = pl.pallas_call(
        kernel,
        out_shape=(
            jax.ShapeDtypeStruct((FEAT, QUARTER), F32),
            jax.ShapeDtypeStruct((2, 2, 2, ROWS, HID), BF16),
        ),
        in_specs=[hbm, vmem, vmem, vmem, vmem, hbm, hbm],
        out_specs=(vmem, vmem),
        scratch_shapes=[
            pltpu.VMEM((TOK, DIN), BF16),
            pltpu.VMEM((TOK, HID), BF16),
            pltpu.VMEM((MSG, NX * TOK), BF16),
            pltpu.VMEM((5, MSG, TOK), BF16),
            pltpu.VMEM((128, NX * TOK), BF16),
            pltpu.VMEM((AUG, TOK), BF16),
            pltpu.VMEM((TOK, 128), BF16),
            pltpu.VMEM((TOK, 128), BF16),
            pltpu.VMEM((AUG, NX * TOK), F32),
            pltpu.VMEM((3, FEAT, TOK), BF16),
            pltpu.VMEM((3, FEAT, TOK), BF16),
            pltpu.VMEM((4, FEAT, QUARTER), F32),
            pltpu.VMEM((3, FEAT, QUARTER), F32),
            pltpu.VMEM((4, FEAT, QUARTER), BF16),
            pltpu.VMEM((FEAT, TOK), BF16),
            pltpu.VMEM((2, ROWS, HID), BF16),
            pltpu.VMEM((7, ROWS, 128), BF16),
            pltpu.VMEM((NZ, 32, 128), BF16),
            pltpu.VMEM((7, 32, 128), BF16),
            pltpu.VMEM((ROWS, 128), BF16),
            pltpu.SemaphoreType.DMA((8,)),
            pltpu.SemaphoreType.DMA((57,)),
            pltpu.SemaphoreType.DMA((57,)),
        ],
        compiler_params=pltpu.CompilerParams(
            collective_id=1, has_side_effects=True, vmem_limit_bytes=56 << 20
        ),
        name="trace_term",
    )(points, w_in, b_in[None, :], w_out, inv_scale[:, None], solves, probes)
    parts = table.reshape(4, 2, ROWS, HID)
    grad_w_in = parts[:, :, :128, :].reshape(DIN, HID).astype(F32)
    grad_b_in = parts[0, 1, 128, :].astype(F32)
    grad_w_out = parts[:, 0, 128:, :].reshape(FEAT, HID).T.astype(F32)
    return feat_grad, grad_w_in, grad_b_in, grad_w_out


def solution(mesh):
    in_specs = (P("blk", None), P(), P(), P(), P(), P(None, "blk"), P(None, "blk"))
    out_specs = (P(None, ("blk", "rep")), P(), P(), P())
    return jax.shard_map(
        on_device, mesh=mesh, in_specs=in_specs, out_specs=out_specs, check_vma=False
    )
```

```python
import math

import jax
import jax.numpy as jnp
from jax import lax
from jax.experimental import pallas as pl
from jax.experimental.pallas import tpu as pltpu
from jax.sharding import PartitionSpec as P

MESH = pl.DeviceIdType.MESH
F32 = jnp.float32
BF16 = jnp.bfloat16
DIN, HID, FEAT, TOK, QUARTER = 1024, 512, 64, 768, 192
HALF = TOK // 2
NX, NZ = 4, 8
ROWS = 144
MSG = 192
AUG = 80
NPTS = 49152


def dot(a, b, ca, cb):
    return lax.dot_general(a, b, (((ca,), (cb,)), ((), ())), preferred_element_type=F32)


def place():
    blk = lax.axis_index("blk")
    rep = lax.axis_index("rep")
    x = lax.rem(blk, NX)
    z = lax.rem(lax.div(blk, NX), NZ)
    y_lo = lax.div(blk, NX * NZ)
    return x, z, y_lo, lax.div(rep, 2), lax.rem(rep, 2)


def device(x, z, y_lo, y_hi, c):
    return ((y_lo * NZ + z) * NX + x, y_hi * 2 + c)


def aligned(start, size, step):
    return pl.ds(pl.multiple_of(start, step), size)


def norm_rows(y, ones_first):
    y32 = y.astype(F32)
    half_sq = -0.5 * jnp.sum(y32 * y32, axis=0, keepdims=True)
    high = half_sq.astype(BF16).astype(F32)
    mid = (half_sq - high).astype(BF16).astype(F32)
    low = (half_sq - high - mid).astype(BF16).astype(F32)
    row = lax.broadcasted_iota(jnp.int32, (16, y.shape[1]), 0)
    base = 3 if ones_first else 0
    ones = 0 if ones_first else 3
    rows = jnp.where((row >= ones) & (row < ones + 3), 1.0, 0.0)
    rows = jnp.where(row == base, high, rows)
    rows = jnp.where(row == base + 1, mid, rows)
    rows = jnp.where(row == base + 2, low, rows)
    return rows.astype(BF16)


def kernel(
    points_in, w_in, b_in, w_t, scale_row, solves, probes,
    feat_out, w_in_out, b_in_out, w_out_out,
    points, hidden, slope, slab_t, own, vis, left, vis_b, vis_y, vis_q, acc,
    half_mine, half_out, half_in, part_out, part_in, halves, grad, msg, recv_a, stage_b, recv_b, chunk, table,
    load_sem, send_sem, recv_sem,
):
    x, z, y_lo, y_hi, c = place()
    rep = y_hi * 2 + c
    step = 1 - 2 * c
    y_vis = y_lo + y_hi - 2 * y_lo * y_hi
    x_next = lax.rem(x + step + NX, NX)
    x_prev = lax.rem(x - step + NX, NX)
    x_far = lax.rem(x + 2, NX)
    z_next = lax.rem(z + step + NZ, NZ)
    z_prev = lax.rem(z - step + NZ, NZ)
    twin = device(x, z, y_lo, y_hi, 1 - c)
    next_z = device(x, z_next, y_lo, y_hi, c)
    near = [device(one, z, y_lo, y_hi, c) for one in (x_next, x_prev, x_far)]
    near += [device(x, one, y_lo, y_hi, c) for one in (z_next, z_prev)]
    near += [device(x, one, 1 - y_lo, y_hi, c) for one in (z, z_next, z_prev)]
    near += [twin, device(x, z, y_lo, 1 - y_hi, c)]

    def lanes(index):
        return aligned(index * TOK, TOK, TOK)

    started = []

    def copy(at, src, dst, peer):
        return pltpu.make_async_remote_copy(
            src_ref=src,
            dst_ref=dst,
            send_sem=send_sem.at[at],
            recv_sem=recv_sem.at[at],
            device_id=peer,
            device_id_type=MESH,
        )

    def send(at, src, dst, peer):
        one = copy(at, src, dst, peer)
        one.start()
        started.append(one)
        return one

    def load(at, src, dst):
        return pltpu.make_async_copy(src, dst, load_sem.at[at])

    barrier = pltpu.get_barrier_semaphore()
    for peer in near:
        pl.semaphore_signal(barrier, inc=1, device_id=peer, device_id_type=MESH)
    loads = []
    for i in range(4):
        part = slice(i * QUARTER, (i + 1) * QUARTER)
        loads.append(load(i, points_in.at[part], points.at[part]))
    loads.append(load(4, solves, own.at[FEAT : 2 * FEAT, lanes(x)]))
    loads.append(load(5, probes, own.at[2 * FEAT : MSG, lanes(x)]))
    for one in loads:
        one.start()

    def features(i):
        part = slice(i * QUARTER, (i + 1) * QUARTER)
        loads[i].wait()
        pre = dot(points[part], w_in[...], 1, 0) + b_in[...]
        hidden[part] = jnp.tanh(pre).astype(BF16)

    features(0)
    loads[4].wait()
    loads[5].wait()
    pl.semaphore_wait(barrier, len(near))

    pairs = slice(FEAT, MSG)
    feats = slice(0, FEAT)
    first_half = aligned(c * HALF, HALF, HALF)
    one_side = aligned(FEAT + c * FEAT, FEAT, FEAT)
    x_peers = [device(lax.rem(x + k, NX), z, y_lo, y_hi, c) for k in range(1, 4)]
    visited = device(x, z_next, y_vis, y_hi, c)

    def to_vis(kind, rows):
        return copy(8 + kind, own.at[rows, lanes(x)], vis.at[1, rows], visited)

    def to_base(kind, rows):
        at = aligned(x * TOK + c * HALF, HALF, HALF)
        return copy(10 + kind, own.at[rows, at], vis.at[0, rows, first_half], device(x, z, 1 - y_lo, y_hi, c))

    def to_z(kind, rows, hop):
        return copy(12 + 2 * hop + kind, vis.at[hop, rows], vis.at[hop + 1, rows], next_z)

    def to_z_last(kind, rows):
        return copy(18 + kind, vis.at[3, rows, first_half], vis.at[4, rows, first_half], next_z)

    started.append(to_vis(0, pairs))
    started[-1].start()
    pair_x = []
    for k in (1, 3, 2):
        part = own.at[one_side, lanes(x)]
        pair_x.append((k, send(20 + k, part, part, x_peers[k - 1])))

    @pl.when(y_hi == 1)
    def _():
        to_base(0, pairs).start()

    for i in range(1, 4):
        features(i)
    scale_row_v = scale_row[...]
    eye = lax.broadcasted_iota(jnp.int32, (FEAT, FEAT), 0) == lax.broadcasted_iota(jnp.int32, (FEAT, FEAT), 1)
    scale = jnp.sum(jnp.where(eye, scale_row_v, 0.0), axis=1, keepdims=True)
    scaled = (dot(w_t[...], hidden[...], 1, 1) * scale).astype(BF16)
    own[feats, lanes(x)] = scaled
    started.append(to_vis(1, feats))
    started[-1].start()

    @pl.when(y_hi == 1)
    def _():
        to_base(1, feats).start()

    feat_x = []
    for k in (1, 3, 2):
        part = own.at[feats, lanes(x)]
        feat_x.append((k, send(24 + k, part, part, x_peers[k - 1])))

    @pl.when(y_hi == 0)
    def _():
        vis[0, :, first_half] = own[:, aligned(x * TOK + c * HALF, HALF, HALF)]

    def ready(index):
        y = own[feats, lanes(index)]
        left[feats, lanes(index)] = y
        left[FEAT:AUG, lanes(index)] = norm_rows(y, False)
        left[AUG:128, lanes(index)] = jnp.zeros((128 - AUG, TOK), BF16)

    def derive(slot, first, size, at):
        cols = aligned(first, size, HALF)
        y = vis[slot, feats, cols]
        augmented = jnp.concatenate([y, norm_rows(y, True)], axis=0)
        vis_b[:, at : at + size] = augmented
        padded = jnp.concatenate([augmented, jnp.zeros((128 - AUG, size), BF16)], axis=0)
        vis_y[at : at + size, :] = padded.T
        swapped = jnp.concatenate([vis[slot, 2 * FEAT : MSG, cols], vis[slot, FEAT : 2 * FEAT, cols]], axis=0)
        vis_q[at : at + size, :] = swapped.T

    def couple(i, at, size):
        span = slice(at, at + size)
        exponent = dot(vis_y[span, :], left[:, i], 1, 0)
        coupling = dot(vis_q[span, :], own[pairs, i], 1, 0)
        weight = (coupling * jnp.exp(exponent)).astype(BF16)
        return dot(vis_b[:, span], weight, 1, 0)

    ready(x)
    slab_t[...] = points[:, aligned(rep * 256, 256, 256)].T

    @pl.when(y_hi == 1)
    def _():
        to_base(0, pairs).wait_recv()
        to_base(1, feats).wait_recv()

    derive(0, c * HALF, HALF, 0)
    acc[:, lanes(x)] = couple(lanes(x), 0, HALF)
    twins = []
    for k, one in pair_x:
        one.wait_recv()
        part = own.at[one_side, lanes(lax.rem(x + NX - k, NX))]
        twins.append(send(28 + k, part, part, twin))
    h32 = hidden[...].astype(F32)
    slope[...] = 1.0 - h32 * h32
    to_vis(0, pairs).wait_recv()
    to_z(0, pairs, 1).start()
    to_vis(1, feats).wait_recv()
    to_z(1, feats, 1).start()
    derive(1, 0, TOK, HALF)
    acc[:, lanes(x)] += couple(lanes(x), HALF, TOK)
    for (k, one), mate in zip(feat_x, twins):
        one.wait_recv()
        mate.wait_recv()
        index = lax.rem(x + NX - k, NX)
        ready(index)

    def first_tiles(k, carry):
        i = lanes(lax.rem(x + k, NX))
        acc[:, i] = couple(i, 0, HALF + TOK)
        return carry

    lax.fori_loop(1, NX, first_tiles, 0)
    to_z(0, pairs, 1).wait_recv()
    to_z(1, feats, 1).wait_recv()
    to_z(0, pairs, 2).start()
    to_z(1, feats, 2).start()
    derive(2, 0, TOK, 0)

    def second_tiles(k, carry):
        i = aligned(k * 2 * TOK, 2 * TOK, 2 * TOK)
        acc[:, i] += couple(i, 0, TOK)
        return carry

    lax.fori_loop(0, 2, second_tiles, 0)
    to_z(0, pairs, 2).wait_recv()
    to_z(1, feats, 2).wait_recv()
    to_z_last(0, pairs).start()
    to_z_last(1, feats).start()
    derive(3, 0, TOK, 0)
    to_z_last(0, pairs).wait_recv()
    to_z_last(1, feats).wait_recv()
    derive(4, c * HALF, HALF, TOK)

    half_twin = {}
    parts = []

    def finish(k):
        index = lax.rem(x + k, NX)
        i = lanes(index)
        pull = acc[:, i] + couple(i, 0, TOK + HALF)
        drift = pull[feats] - own[feats, i].astype(F32) * pull[FEAT : FEAT + 1]
        quarter = [drift[:, q * QUARTER : (q + 1) * QUARTER] for q in range(4)]
        first = c == 0
        half_mine[k, :, 0:QUARTER] = jnp.where(first, quarter[0], quarter[1])
        half_mine[k, :, QUARTER:HALF] = jnp.where(first, quarter[2], quarter[3])
        half_out[k, :, 0:QUARTER] = jnp.where(first, quarter[1], quarter[0]).astype(BF16)
        half_out[k, :, QUARTER:HALF] = jnp.where(first, quarter[3], quarter[2]).astype(BF16)
        half_twin[k] = send(32 + k, half_out.at[k], half_in.at[k], twin)

    def pass_on(k):
        half_twin[k].wait_recv()
        part = half_mine[k] + half_in[k].astype(F32)
        part_out[k] = part.astype(BF16)
        index = lax.rem(x + k, NX)
        if k:
            parts.append(send(36 + k, part_out.at[k], part_in.at[k], device(index, z, y_lo, y_hi, c)))
        parts.append(send(40 + k, part_out.at[k], part_in.at[4 + k], device(index, z, y_lo, 1 - y_hi, c)))
        return part

    finish(2)
    finish(1)
    pass_on(2)
    finish(3)
    pass_on(1)
    finish(0)
    pass_on(3)
    total = pass_on(0)
    for one in parts:
        one.wait_recv()
    for k in range(1, 8):
        total = total + part_in[k].astype(F32)
    total = total * scale
    feat_out[...] = jnp.where(y_hi == 0, total[:, 0:QUARTER], total[:, QUARTER:HALF])
    halves[c] = total.astype(BF16)
    send(44, halves.at[c], halves.at[c], twin).wait_recv()
    for q in range(4):
        at = (q // 2) * QUARTER
        grad[:, q * QUARTER : (q + 1) * QUARTER] = halves[q % 2, :, at : at + QUARTER]

    norm = 1.0 / math.sqrt(NPTS)
    pre = dot(grad[...], w_t[...], 0, 0) * slope[...]
    gw = dot(slab_t[...], pre.astype(BF16), 1, 0) * norm
    bias = jnp.sum(pre, axis=0, keepdims=True) * norm
    gwo = dot(grad[aligned(rep * 16, 16, 16), :], hidden[...], 1, 0) * norm
    msg[0, 0:128, :] = gw[0:128].astype(BF16)
    msg[1, 0:128, :] = gw[128:256].astype(BF16)
    msg[0, 128:144, :] = gwo.astype(BF16)
    msg[1, 128:144, :] = jnp.broadcast_to(bias, (16, HID)).astype(BF16)

    def strip(px):
        return aligned(px * 128, 128, 128)

    cell = y_lo * NX + x
    plane = []
    column = []
    for d in range(1, 8):
        other = lax.rem(cell + d, 8)
        plane.append((lax.rem(other, NX), lax.div(other, NX)))
        column.append(lax.rem(z + d, NZ))
    arrivals = []
    for d in range(1, 8):
        px, py = plane[d - 1]
        arrivals.append(send(44 + d, msg.at[py, :, strip(px)], recv_a.at[d - 1], device(px, z, py, y_hi, c)))
    summed = msg[y_lo, :, strip(x)].astype(F32)
    for d in range(1, 8):
        arrivals[d - 1].wait_recv()
        summed = summed + recv_a[d - 1].astype(F32)
    summed_b = summed.astype(BF16)
    for b in range(NZ):
        stage_b[b, 0:16, :] = summed_b[b * 16 : b * 16 + 16]
        stage_b[b, 16:32, :] = summed_b[128:144]
    arrivals = []
    for d in (4, 3, 5, 2, 6, 1, 7):
        pz = column[d - 1]
        arrivals.append(send(51 + d, stage_b.at[pz], recv_b.at[d - 1], device(x, pz, y_lo, y_hi, c)))
    for one in arrivals:
        one.wait_recv()
    tile = stage_b[z].astype(F32)
    for d in range(1, 8):
        tile = tile + recv_b[d - 1].astype(F32)
    tile_b = tile.astype(BF16)
    band = aligned(z * 16, 16, 16)
    chunk[band, :] = tile_b[0:16]
    chunk[128:144, :] = tile_b[16:32]
    arrivals = []
    for d in (4, 3, 5, 2, 6, 1, 7):
        pz = column[d - 1]
        arrivals.append(send(58 + d, chunk.at[band], chunk.at[band], device(x, pz, y_lo, y_hi, c)))
    for one in arrivals:
        one.wait_recv()
    place_mine = table.at[y_hi, c, y_lo, :, strip(x)]
    groups = []
    for dh in range(2):
        for dl in range(2):
            hi = y_hi + dh - 2 * y_hi * dh
            lo = y_lo + dl - 2 * y_lo * dl
            groups.append((dh, dl, hi, lo, []))
    for dx in (2, 1, 3, 0):
        for dh, dl, hi, lo, got in groups[::-1]:
            if dh or dl or dx:
                at = 65 + dh * 8 + dl * 4 + dx
                peer = device(lax.rem(x + dx, NX), z, lo, hi, c)
                got.append(send(at, chunk, place_mine, peer))
    table[y_hi, c, y_lo, :, strip(x)] = chunk[...]
    shared = []
    for dh, dl, hi, lo, got in groups:
        for one in got:
            one.wait_recv()
        part = table.at[hi, c, lo]
        shared.append(send(82 + dh * 2 + dl, part, part, twin))
    for h in range(2):
        for half in range(2):
            row = (h * 2 + c) * 256 + half * 128
            w_in_out[aligned(row, 128, 128), :] = table[h, c, half, 0:128, :]
    for one in shared:
        one.wait_recv()
    for h in range(2):
        for half in range(2):
            row = (h * 2 + 1 - c) * 256 + half * 128
            w_in_out[aligned(row, 128, 128), :] = table[h, 1 - c, half, 0:128, :]
    b_in_out[...] = table[0, 0, 1, 128:144, :].astype(F32)[0:1]
    for q in range(4):
        w_out_out[q * 16 : q * 16 + 16, :] = table[q // 2, q % 2, 0, 128:144, :].astype(F32)
    for one in started:
        one.wait_send()
    for hop in (1, 2):
        to_z(0, pairs, hop).wait_send()
        to_z(1, feats, hop).wait_send()
    to_z_last(0, pairs).wait_send()
    to_z_last(1, feats).wait_send()

    @pl.when(y_hi == 1)
    def _():
        to_base(0, pairs).wait_send()
        to_base(1, feats).wait_send()


def on_device(points, w_in, b_in, w_out, inv_scale, solves, probes):
    vmem = pl.BlockSpec(memory_space=pltpu.VMEM)
    hbm = pl.BlockSpec(memory_space=pl.ANY)
    feat_grad, grad_w_in, grad_b_in, grad_w_out = pl.pallas_call(
        kernel,
        out_shape=(
            jax.ShapeDtypeStruct((FEAT, QUARTER), F32),
            jax.ShapeDtypeStruct((DIN, HID), BF16),
            jax.ShapeDtypeStruct((1, HID), F32),
            jax.ShapeDtypeStruct((FEAT, HID), F32),
        ),
        in_specs=[hbm, vmem, vmem, vmem, vmem, hbm, hbm],
        out_specs=(vmem, vmem, vmem, vmem),
        scratch_shapes=[
            pltpu.VMEM((TOK, DIN), BF16),
            pltpu.VMEM((TOK, HID), BF16),
            pltpu.VMEM((TOK, HID), F32),
            pltpu.VMEM((256, TOK), BF16),
            pltpu.VMEM((MSG, NX * TOK), BF16),
            pltpu.VMEM((5, MSG, TOK), BF16),
            pltpu.VMEM((128, NX * TOK), BF16),
            pltpu.VMEM((AUG, TOK + HALF), BF16),
            pltpu.VMEM((TOK + HALF, 128), BF16),
            pltpu.VMEM((TOK + HALF, 128), BF16),
            pltpu.VMEM((AUG, NX * TOK), F32),
            pltpu.VMEM((4, FEAT, HALF), F32),
            pltpu.VMEM((4, FEAT, HALF), BF16),
            pltpu.VMEM((4, FEAT, HALF), BF16),
            pltpu.VMEM((4, FEAT, HALF), BF16),
            pltpu.VMEM((8, FEAT, HALF), BF16),
            pltpu.VMEM((2, FEAT, HALF), BF16),
            pltpu.VMEM((FEAT, TOK), BF16),
            pltpu.VMEM((2, ROWS, HID), BF16),
            pltpu.VMEM((7, ROWS, 128), BF16),
            pltpu.VMEM((NZ, 32, 128), BF16),
            pltpu.VMEM((7, 32, 128), BF16),
            pltpu.VMEM((ROWS, 128), BF16),
            pltpu.VMEM((2, 2, 2, ROWS, HID), BF16),
            pltpu.SemaphoreType.DMA((6,)),
            pltpu.SemaphoreType.DMA((86,)),
            pltpu.SemaphoreType.DMA((86,)),
        ],
        compiler_params=pltpu.CompilerParams(
            collective_id=1, has_side_effects=True, vmem_limit_bytes=56 << 20
        ),
        name="trace_term",
    )(points, w_in, b_in[None, :], w_out.T, inv_scale[None, :], solves, probes)
    return feat_grad, grad_w_in.astype(F32), grad_b_in[0], grad_w_out.T


def solution(mesh):
    in_specs = (P("blk", None), P(), P(), P(), P(), P(None, "blk"), P(None, "blk"))
    out_specs = (P(None, ("blk", "rep")), P(), P(), P())
    return jax.shard_map(
        on_device, mesh=mesh, in_specs=in_specs, out_specs=out_specs, check_vma=False
    )
```

```python
import math

import jax
import jax.numpy as jnp
from jax import lax
from jax.experimental import pallas as pl
from jax.experimental.pallas import tpu as pltpu
from jax.sharding import PartitionSpec as P

MESH = pl.DeviceIdType.MESH
F32 = jnp.float32
BF16 = jnp.bfloat16
DIN, HID, FEAT, TOK, QUARTER = 1024, 512, 64, 768, 192
HALF = TOK // 2
NX, NZ = 4, 8
ROWS = 144
MSG = 192
AUG = 80
NPTS = 49152


def dot(a, b, ca, cb):
    return lax.dot_general(a, b, (((ca,), (cb,)), ((), ())), preferred_element_type=F32)


def place():
    blk = lax.axis_index("blk")
    rep = lax.axis_index("rep")
    x = lax.rem(blk, NX)
    z = lax.rem(lax.div(blk, NX), NZ)
    y_lo = lax.div(blk, NX * NZ)
    return x, z, y_lo, lax.div(rep, 2), lax.rem(rep, 2)


def device(x, z, y_lo, y_hi, c):
    return ((y_lo * NZ + z) * NX + x, y_hi * 2 + c)


def aligned(start, size, step):
    return pl.ds(pl.multiple_of(start, step), size)


def norm_rows(y, ones_first):
    y32 = y.astype(F32)
    half_sq = -0.5 * jnp.sum(y32 * y32, axis=0, keepdims=True)
    high = half_sq.astype(BF16).astype(F32)
    mid = (half_sq - high).astype(BF16).astype(F32)
    low = (half_sq - high - mid).astype(BF16).astype(F32)
    row = lax.broadcasted_iota(jnp.int32, (16, y.shape[1]), 0)
    base = 3 if ones_first else 0
    ones = 0 if ones_first else 3
    rows = jnp.where((row >= ones) & (row < ones + 3), 1.0, 0.0)
    rows = jnp.where(row == base, high, rows)
    rows = jnp.where(row == base + 1, mid, rows)
    rows = jnp.where(row == base + 2, low, rows)
    return rows.astype(BF16)


def kernel(
    points_in, w_in_any, b_in, w_t, scale_row, solves, probes,
    feat_out, w_in_out, b_in_out, w_out_out,
    points, w_in, hidden, slope, slab_t, own, vis, left, vis_b, vis_y, vis_q, acc,
    half_mine, half_out, half_in, part_out, part_in, halves, grad, msg, recv_a, stage_b, recv_b, chunk, table,
    load_sem, send_sem, recv_sem, out_sem,
):
    x, z, y_lo, y_hi, c = place()
    rep = y_hi * 2 + c
    step = 1 - 2 * c
    y_vis = y_lo + y_hi - 2 * y_lo * y_hi
    x_next = lax.rem(x + step + NX, NX)
    x_prev = lax.rem(x - step + NX, NX)
    x_far = lax.rem(x + 2, NX)
    z_next = lax.rem(z + step + NZ, NZ)
    z_prev = lax.rem(z - step + NZ, NZ)
    twin = device(x, z, y_lo, y_hi, 1 - c)
    next_z = device(x, z_next, y_lo, y_hi, c)
    near = [device(one, z, y_lo, y_hi, c) for one in (x_next, x_prev, x_far)]
    near += [device(x, one, y_lo, y_hi, c) for one in (z_next, z_prev)]
    near += [device(x, one, 1 - y_lo, y_hi, c) for one in (z, z_next, z_prev)]
    near += [twin, device(x, z, y_lo, 1 - y_hi, c)]

    def lanes(index):
        return aligned(index * TOK, TOK, TOK)

    started = []

    def copy(at, src, dst, peer):
        return pltpu.make_async_remote_copy(
            src_ref=src,
            dst_ref=dst,
            send_sem=send_sem.at[at],
            recv_sem=recv_sem.at[at],
            device_id=peer,
            device_id_type=MESH,
        )

    def send(at, src, dst, peer):
        one = copy(at, src, dst, peer)
        one.start()
        started.append(one)
        return one

    def load(at, src, dst):
        return pltpu.make_async_copy(src, dst, load_sem.at[at])

    barrier = pltpu.get_barrier_semaphore()
    for peer in near:
        pl.semaphore_signal(barrier, inc=1, device_id=peer, device_id_type=MESH)
    loads = []
    for i in range(4):
        part = slice(i * QUARTER, (i + 1) * QUARTER)
        loads.append(load(i, points_in.at[part], points.at[part]))
    loads.insert(0, load(6, w_in_any, w_in))
    loads.append(load(4, solves, own.at[FEAT : 2 * FEAT, lanes(x)]))
    loads.append(load(5, probes, own.at[2 * FEAT : MSG, lanes(x)]))
    for one in loads:
        one.start()

    def features(i):
        part = slice(i * QUARTER, (i + 1) * QUARTER)
        loads[i + 1].wait()
        pre = dot(points[part], w_in[...], 1, 0) + b_in[...]
        hidden[part] = jnp.tanh(pre).astype(BF16)

    loads[5].wait()
    loads[6].wait()
    loads[0].wait()
    features(0)
    pl.semaphore_wait(barrier, len(near))

    pairs = slice(FEAT, MSG)
    feats = slice(0, FEAT)
    first_half = aligned(c * HALF, HALF, HALF)
    one_side = aligned(FEAT + c * FEAT, FEAT, FEAT)
    x_peers = [device(lax.rem(x + k, NX), z, y_lo, y_hi, c) for k in range(1, 4)]
    visited = device(x, z_next, y_vis, y_hi, c)

    pieces = [slice(FEAT, 2 * FEAT), slice(2 * FEAT, MSG), feats]
    vectors = (0, 1)
    everything = (0, 1, 2)

    def to_vis(n):
        return copy(n, own.at[pieces[n], lanes(x)], vis.at[1, pieces[n]], visited)

    def to_base(n):
        at = aligned(x * TOK + c * HALF, HALF, HALF)
        return copy(3 + n, own.at[pieces[n], at], vis.at[0, pieces[n], first_half], device(x, z, 1 - y_lo, y_hi, c))

    def to_z(hop, n):
        at = 6 + 3 * (hop - 1) + n
        if hop < 3:
            return copy(at, vis.at[hop, pieces[n]], vis.at[hop + 1, pieces[n]], next_z)
        part = (pieces[n], first_half)
        return copy(at, vis.at[3, *part], vis.at[4, *part], next_z)

    def pump(hop, which):
        for n in which:
            (to_vis(n) if hop == 1 else to_z(hop - 1, n)).wait_recv()
            if hop < 4:
                started.append(to_z(hop, n))
                started[-1].start()

    @pl.when(y_hi == 1)
    def _():
        for n in vectors:
            to_base(n).start()

    for n in vectors:
        started.append(to_vis(n))
        started[-1].start()
    pair_x = {}
    feat_x = {}
    twins = {}

    def send_pair(k):
        part = own.at[one_side, lanes(x)]
        pair_x[k] = send(20 + k, part, part, x_peers[k - 1])

    def send_feat(k):
        part = own.at[feats, lanes(x)]
        feat_x[k] = send(24 + k, part, part, x_peers[k - 1])

    def share_pair(k):
        pair_x[k].wait_recv()
        part = own.at[one_side, lanes(lax.rem(x + NX - k, NX))]
        twins[k] = send(28 + k, part, part, twin)

    send_pair(1)
    send_pair(3)
    for i in range(1, 4):
        features(i)
    scale_row_v = scale_row[...]
    eye = lax.broadcasted_iota(jnp.int32, (FEAT, FEAT), 0) == lax.broadcasted_iota(jnp.int32, (FEAT, FEAT), 1)
    scale = jnp.sum(jnp.where(eye, scale_row_v, 0.0), axis=1, keepdims=True)
    scaled = (dot(w_t[...], hidden[...], 1, 1) * scale).astype(BF16)
    own[feats, lanes(x)] = scaled
    @pl.when(y_hi == 1)
    def _():
        to_base(2).start()

    started.append(to_vis(2))
    started[-1].start()
    send_feat(1)
    send_feat(3)
    send_pair(2)
    send_feat(2)

    @pl.when(y_hi == 0)
    def _():
        vis[0, :, first_half] = own[:, aligned(x * TOK + c * HALF, HALF, HALF)]

    def ready(index):
        y = own[feats, lanes(index)]
        left[feats, lanes(index)] = y
        left[FEAT:AUG, lanes(index)] = norm_rows(y, False)
        left[AUG:128, lanes(index)] = jnp.zeros((128 - AUG, TOK), BF16)

    def derive(slot, first, size, at):
        cols = aligned(first, size, HALF)
        y = vis[slot, feats, cols]
        augmented = jnp.concatenate([y, norm_rows(y, True)], axis=0)
        vis_b[:, at : at + size] = augmented
        padded = jnp.concatenate([augmented, jnp.zeros((128 - AUG, size), BF16)], axis=0)
        vis_y[at : at + size, :] = padded.T
        swapped = jnp.concatenate([vis[slot, 2 * FEAT : MSG, cols], vis[slot, FEAT : 2 * FEAT, cols]], axis=0)
        vis_q[at : at + size, :] = swapped.T

    def couple(i, at, size):
        span = slice(at, at + size)
        exponent = dot(vis_y[span, :], left[:, i], 1, 0)
        coupling = dot(vis_q[span, :], own[pairs, i], 1, 0)
        weight = (coupling * jnp.exp(exponent)).astype(BF16)
        return dot(vis_b[:, span], weight, 1, 0)

    def meet(k):
        feat_x[k].wait_recv()
        twins[k].wait_recv()
        index = lax.rem(x + NX - k, NX)
        ready(index)
        acc[:, lanes(index)] = couple(lanes(index), 0, HALF + TOK)

    ready(x)
    slab_t[...] = points[:, aligned(rep * 256, 256, 256)].T
    h32 = hidden[...].astype(F32)
    slope[...] = 1.0 - h32 * h32

    @pl.when(y_hi == 1)
    def _():
        for n in everything:
            to_base(n).wait_recv()

    derive(0, c * HALF, HALF, 0)
    acc[:, lanes(x)] = couple(lanes(x), 0, HALF)
    share_pair(1)
    share_pair(3)
    pump(1, everything)
    derive(1, 0, TOK, HALF)
    acc[:, lanes(x)] += couple(lanes(x), HALF, TOK)
    share_pair(2)
    meet(1)
    pump(2, vectors)
    meet(3)
    pump(2, (2,))
    meet(2)
    derive(2, 0, TOK, 0)

    def second_tiles(k):
        i = aligned(k * 2 * TOK, 2 * TOK, 2 * TOK)
        acc[:, i] += couple(i, 0, TOK)

    second_tiles(0)
    pump(3, everything)
    second_tiles(1)
    derive(3, 0, TOK, 0)
    pump(4, everything)
    derive(4, c * HALF, HALF, TOK)

    half_twin = {}
    parts = []

    def finish(k):
        index = lax.rem(x + k, NX)
        i = lanes(index)
        pull = acc[:, i] + couple(i, 0, TOK + HALF)
        drift = pull[feats] - own[feats, i].astype(F32) * pull[FEAT : FEAT + 1]
        quarter = [drift[:, q * QUARTER : (q + 1) * QUARTER] for q in range(4)]
        first = c == 0
        half_mine[k, :, 0:QUARTER] = jnp.where(first, quarter[0], quarter[1])
        half_mine[k, :, QUARTER:HALF] = jnp.where(first, quarter[2], quarter[3])
        half_out[k, :, 0:QUARTER] = jnp.where(first, quarter[1], quarter[0]).astype(BF16)
        half_out[k, :, QUARTER:HALF] = jnp.where(first, quarter[3], quarter[2]).astype(BF16)
        half_twin[k] = send(32 + k, half_out.at[k], half_in.at[k], twin)

    def pass_on(k):
        half_twin[k].wait_recv()
        part = half_mine[k] + half_in[k].astype(F32)
        part_out[k] = part.astype(BF16)
        index = lax.rem(x + k, NX)
        if k:
            parts.append(send(36 + k, part_out.at[k], part_in.at[k], device(index, z, y_lo, y_hi, c)))
        parts.append(send(40 + k, part_out.at[k], part_in.at[4 + k], device(index, z, y_lo, 1 - y_hi, c)))
        return part

    finish(2)
    finish(1)
    pass_on(2)
    finish(3)
    pass_on(1)
    finish(0)
    pass_on(3)
    total = pass_on(0)
    for one in parts:
        one.wait_recv()
    for k in range(1, 8):
        total = total + part_in[k].astype(F32)
    total = total * scale
    feat_out[...] = jnp.where(y_hi == 0, total[:, 0:QUARTER], total[:, QUARTER:HALF])
    halves[c] = total.astype(BF16)
    send(44, halves.at[c], halves.at[c], twin).wait_recv()
    for q in range(4):
        at = (q // 2) * QUARTER
        grad[:, q * QUARTER : (q + 1) * QUARTER] = halves[q % 2, :, at : at + QUARTER]

    norm = 1.0 / math.sqrt(NPTS)
    pre = dot(grad[...], w_t[...], 0, 0) * slope[...]
    gw = dot(slab_t[...], pre.astype(BF16), 1, 0) * norm
    bias = jnp.sum(pre, axis=0, keepdims=True) * norm
    gwo = dot(grad[aligned(rep * 16, 16, 16), :], hidden[...], 1, 0) * norm
    msg[0, 0:128, :] = gw[0:128].astype(BF16)
    msg[1, 0:128, :] = gw[128:256].astype(BF16)
    msg[0, 128:144, :] = gwo.astype(BF16)
    msg[1, 128:144, :] = jnp.broadcast_to(bias, (16, HID)).astype(BF16)

    def strip(px):
        return aligned(px * 128, 128, 128)

    cell = y_lo * NX + x
    plane = []
    column = []
    for d in range(1, 8):
        other = lax.rem(cell + d, 8)
        plane.append((lax.rem(other, NX), lax.div(other, NX)))
        column.append(lax.rem(z + d, NZ))
    arrivals = []
    for d in range(1, 8):
        px, py = plane[d - 1]
        arrivals.append(send(44 + d, msg.at[py, :, strip(px)], recv_a.at[d - 1], device(px, z, py, y_hi, c)))
    summed = msg[y_lo, :, strip(x)].astype(F32)
    for d in range(1, 8):
        arrivals[d - 1].wait_recv()
        summed = summed + recv_a[d - 1].astype(F32)
    summed_b = summed.astype(BF16)
    for b in range(NZ):
        stage_b[b, 0:16, :] = summed_b[b * 16 : b * 16 + 16]
        stage_b[b, 16:32, :] = summed_b[128:144]
    arrivals = []
    for d in (4, 3, 5, 2, 6, 1, 7):
        pz = column[d - 1]
        arrivals.append(send(51 + d, stage_b.at[pz], recv_b.at[d - 1], device(x, pz, y_lo, y_hi, c)))
    for one in arrivals:
        one.wait_recv()
    tile = stage_b[z].astype(F32)
    for d in range(1, 8):
        tile = tile + recv_b[d - 1].astype(F32)
    tile_b = tile.astype(BF16)
    band = aligned(z * 16, 16, 16)
    chunk[band, :] = tile_b[0:16]
    chunk[128:144, :] = tile_b[16:32]
    arrivals = []
    for d in (4, 3, 5, 2, 6, 1, 7):
        pz = column[d - 1]
        arrivals.append(send(58 + d, chunk.at[band], chunk.at[band], device(x, pz, y_lo, y_hi, c)))
    for one in arrivals:
        one.wait_recv()
    place_mine = table.at[y_hi, c, y_lo, :, strip(x)]
    groups = []
    for dh in range(2):
        for dl in range(2):
            hi = y_hi + dh - 2 * y_hi * dh
            lo = y_lo + dl - 2 * y_lo * dl
            groups.append((dh, dl, hi, lo, []))
    for dx in (2, 1, 3, 0):
        for dh, dl, hi, lo, got in groups[::-1]:
            if dh or dl or dx:
                at = 65 + dh * 8 + dl * 4 + dx
                peer = device(lax.rem(x + dx, NX), z, lo, hi, c)
                got.append(send(at, chunk, place_mine, peer))
    table[y_hi, c, y_lo, :, strip(x)] = chunk[...]
    shared = []
    stores = []

    def store(at, h, core, half):
        row = (h * 2 + core) * 256 + half * 128
        one = pltpu.make_async_copy(table.at[h, core, half, 0:128, :], w_in_out.at[aligned(row, 128, 128), :], out_sem.at[at])
        one.start()
        stores.append(one)

    for n, (dh, dl, hi, lo, got) in enumerate(groups):
        for one in got:
            one.wait_recv()
        part = table.at[hi, c, lo]
        shared.append(send(82 + n, part, part, twin))
        store(n, hi, c, lo)
    for n, (dh, dl, hi, lo, got) in enumerate(groups):
        shared[n].wait_recv()
        store(4 + n, hi, 1 - c, lo)
    b_in_out[...] = table[0, 0, 1, 128:144, :].astype(F32)[0:1]
    for q in range(4):
        w_out_out[q * 16 : q * 16 + 16, :] = table[q // 2, q % 2, 0, 128:144, :].astype(F32)
    for one in started:
        one.wait_send()
    for one in stores:
        one.wait()

    @pl.when(y_hi == 1)
    def _():
        for n in everything:
            to_base(n).wait_send()


def write_kernel(feat, w_in, b_in, w_out, feat_out, w_in_out, b_in_out, w_out_out):
    feat_out[...] = feat[...]
    w_in_out[...] = w_in[...].astype(F32)
    b_in_out[...] = b_in[...]
    w_out_out[...] = w_out[...]


def write(feat, w_in, b_in, w_out):
    specs = []
    for part in (feat, w_in, b_in, w_out):
        if part is w_in:
            specs.append(pl.BlockSpec((DIN // 4, HID), lambda i: (i, 0)))
        else:
            specs.append(pl.BlockSpec(part.shape, lambda i: (0, 0)))
    return pl.pallas_call(
        write_kernel,
        grid=(4,),
        out_shape=tuple(jax.ShapeDtypeStruct(part.shape, F32) for part in (feat, w_in, b_in, w_out)),
        in_specs=specs,
        out_specs=tuple(specs),
        name="write",
    )(feat, w_in, b_in, w_out)


def on_device(points, w_in, b_in, w_out, inv_scale, solves, probes):
    vmem = pl.BlockSpec(memory_space=pltpu.VMEM)
    hbm = pl.BlockSpec(memory_space=pl.ANY)
    parts = pl.pallas_call(
        kernel,
        out_shape=(
            jax.ShapeDtypeStruct((FEAT, QUARTER), F32),
            jax.ShapeDtypeStruct((DIN, HID), BF16),
            jax.ShapeDtypeStruct((1, HID), F32),
            jax.ShapeDtypeStruct((FEAT, HID), F32),
        ),
        in_specs=[hbm, hbm, vmem, vmem, vmem, hbm, hbm],
        out_specs=(vmem, hbm, vmem, vmem),
        scratch_shapes=[
            pltpu.VMEM((TOK, DIN), BF16),
            pltpu.VMEM((DIN, HID), BF16),
            pltpu.VMEM((TOK, HID), BF16),
            pltpu.VMEM((TOK, HID), F32),
            pltpu.VMEM((256, TOK), BF16),
            pltpu.VMEM((MSG, NX * TOK), BF16),
            pltpu.VMEM((5, MSG, TOK), BF16),
            pltpu.VMEM((128, NX * TOK), BF16),
            pltpu.VMEM((AUG, TOK + HALF), BF16),
            pltpu.VMEM((TOK + HALF, 128), BF16),
            pltpu.VMEM((TOK + HALF, 128), BF16),
            pltpu.VMEM((AUG, NX * TOK), F32),
            pltpu.VMEM((4, FEAT, HALF), F32),
            pltpu.VMEM((4, FEAT, HALF), BF16),
            pltpu.VMEM((4, FEAT, HALF), BF16),
            pltpu.VMEM((4, FEAT, HALF), BF16),
            pltpu.VMEM((8, FEAT, HALF), BF16),
            pltpu.VMEM((2, FEAT, HALF), BF16),
            pltpu.VMEM((FEAT, TOK), BF16),
            pltpu.VMEM((2, ROWS, HID), BF16),
            pltpu.VMEM((7, ROWS, 128), BF16),
            pltpu.VMEM((NZ, 32, 128), BF16),
            pltpu.VMEM((7, 32, 128), BF16),
            pltpu.VMEM((ROWS, 128), BF16),
            pltpu.VMEM((2, 2, 2, ROWS, HID), BF16),
            pltpu.SemaphoreType.DMA((7,)),
            pltpu.SemaphoreType.DMA((86,)),
            pltpu.SemaphoreType.DMA((86,)),
            pltpu.SemaphoreType.DMA((8,)),
        ],
        compiler_params=pltpu.CompilerParams(
            collective_id=1, has_side_effects=True, vmem_limit_bytes=56 << 20
        ),
        name="trace_term",
    )(points, w_in, b_in[None, :], w_out.T, inv_scale[None, :], solves, probes)
    feat_grad, grad_w_in, grad_b_in, grad_w_out = write(*parts)
    return feat_grad, grad_w_in, grad_b_in[0], grad_w_out.T


def solution(mesh):
    in_specs = (P("blk", None), P(), P(), P(), P(), P(None, "blk"), P(None, "blk"))
    out_specs = (P(None, ("blk", "rep")), P(), P(), P())
    return jax.shard_map(
        on_device, mesh=mesh, in_specs=in_specs, out_specs=out_specs, check_vma=False
    )
```

```python
import math

import jax
import jax.numpy as jnp
from jax import lax
from jax.experimental import pallas as pl
from jax.experimental.pallas import tpu as pltpu
from jax.sharding import PartitionSpec as P

MESH = pl.DeviceIdType.MESH
F32 = jnp.float32
BF16 = jnp.bfloat16
DIN, HID, FEAT, TOK, QUARTER = 1024, 512, 64, 768, 192
HALF = TOK // 2
NX, NZ = 4, 8
ROWS = 144
MSG = 192
AUG = 80
NPTS = 49152


def dot(a, b, ca, cb):
    return lax.dot_general(a, b, (((ca,), (cb,)), ((), ())), preferred_element_type=F32)


def place():
    blk = lax.axis_index("blk")
    rep = lax.axis_index("rep")
    x = lax.rem(blk, NX)
    z = lax.rem(lax.div(blk, NX), NZ)
    y_lo = lax.div(blk, NX * NZ)
    return x, z, y_lo, lax.div(rep, 2), lax.rem(rep, 2)


def device(x, z, y_lo, y_hi, c):
    return ((y_lo * NZ + z) * NX + x, y_hi * 2 + c)


def aligned(start, size, step):
    return pl.ds(pl.multiple_of(start, step), size)


def norm_rows(y, ones_first):
    y32 = y.astype(F32)
    half_sq = -0.5 * jnp.sum(y32 * y32, axis=0, keepdims=True)
    high = half_sq.astype(BF16).astype(F32)
    mid = (half_sq - high).astype(BF16).astype(F32)
    low = (half_sq - high - mid).astype(BF16).astype(F32)
    row = lax.broadcasted_iota(jnp.int32, (16, y.shape[1]), 0)
    base = 3 if ones_first else 0
    ones = 0 if ones_first else 3
    rows = jnp.where((row >= ones) & (row < ones + 3), 1.0, 0.0)
    rows = jnp.where(row == base, high, rows)
    rows = jnp.where(row == base + 1, mid, rows)
    rows = jnp.where(row == base + 2, low, rows)
    return rows.astype(BF16)


def kernel(
    points_in, w_in_any, b_in, w_t, scale_row, solves, probes,
    feat_out, w_in_out, b_in_out, w_out_out,
    points, w_in, hidden, slope, slab_t, own, held, vis, mate, left, vis_b, vis_y, vis_q, acc,
    half_own, part_out, part_in, halves, grad, msg, recv_a, stage_b, recv_b, chunk, table,
    load_sem, send_sem, recv_sem, out_sem,
):
    x, z, y_lo, y_hi, c = place()
    rep = y_hi * 2 + c
    step = 1 - 2 * c
    y_vis = y_lo + y_hi - 2 * y_lo * y_hi
    x_next = lax.rem(x + step + NX, NX)
    x_prev = lax.rem(x - step + NX, NX)
    x_far = lax.rem(x + 2, NX)
    z_next = lax.rem(z + step + NZ, NZ)
    z_prev = lax.rem(z - step + NZ, NZ)
    twin = device(x, z, y_lo, y_hi, 1 - c)
    next_z = device(x, z_next, y_lo, y_hi, c)
    near = [device(one, z, y_lo, y_hi, c) for one in (x_next, x_prev, x_far)]
    near += [device(x, one, y_lo, y_hi, c) for one in (z_next, z_prev)]
    near += [device(x, one, 1 - y_lo, y_hi, c) for one in (z, z_next, z_prev)]
    near += [twin, device(x, z, y_lo, 1 - y_hi, c)]

    def lanes(index):
        return aligned(index * HALF, HALF, HALF)

    started = []

    def copy(at, src, dst, peer):
        return pltpu.make_async_remote_copy(
            src_ref=src,
            dst_ref=dst,
            send_sem=send_sem.at[at],
            recv_sem=recv_sem.at[at],
            device_id=peer,
            device_id_type=MESH,
        )

    def send(at, src, dst, peer):
        one = copy(at, src, dst, peer)
        one.start()
        started.append(one)
        return one

    def load(at, src, dst):
        return pltpu.make_async_copy(src, dst, load_sem.at[at])

    barrier = pltpu.get_barrier_semaphore()
    for peer in near:
        pl.semaphore_signal(barrier, inc=1, device_id=peer, device_id_type=MESH)
    loads = []
    for i in range(4):
        part = slice(i * QUARTER, (i + 1) * QUARTER)
        loads.append(load(i, points_in.at[part], points.at[part]))
    loads.insert(0, load(6, w_in_any, w_in))
    loads.append(load(4, solves, own.at[FEAT : 2 * FEAT]))
    loads.append(load(5, probes, own.at[2 * FEAT : MSG]))
    for one in loads:
        one.start()

    def features(i):
        part = slice(i * QUARTER, (i + 1) * QUARTER)
        loads[i + 1].wait()
        pre = dot(points[part], w_in[...], 1, 0) + b_in[...]
        hidden[part] = jnp.tanh(pre).astype(BF16)

    loads[5].wait()
    loads[6].wait()
    loads[0].wait()
    features(0)
    pl.semaphore_wait(barrier, len(near))

    pairs = slice(FEAT, MSG)
    feats = slice(0, FEAT)
    pieces = [slice(FEAT, 2 * FEAT), slice(2 * FEAT, MSG), feats]
    vectors = (0, 1)
    everything = (0, 1, 2)
    side = aligned(c * HALF, HALF, HALF)
    x_peers = [device(lax.rem(x + k, NX), z, y_lo, y_hi, c) for k in range(1, 4)]
    visited = device(x, z_next, y_vis, y_hi, c)

    def to_vis(n):
        return copy(n, own.at[pieces[n]], vis.at[1, pieces[n]], visited)

    def to_base(n):
        return copy(3 + n, own.at[pieces[n], side], vis.at[0, pieces[n], side], device(x, z, 1 - y_lo, y_hi, c))

    def share_base(n):
        part = vis.at[0, pieces[n], side]
        return copy(35 + n, part, part, twin)

    def to_z(hop, n):
        at = 6 + 3 * (hop - 1) + n
        if hop < 3:
            return copy(at, vis.at[hop, pieces[n]], vis.at[hop + 1, pieces[n]], next_z)
        return copy(at, vis.at[3, pieces[n], side], vis.at[4, pieces[n], side], next_z)

    def to_mate(hop, n):
        at = 23 + 3 * (hop - 1) + n
        if hop < 4:
            return copy(at, vis.at[hop, pieces[n]], mate.at[hop - 1, pieces[n]], twin)
        part = vis.at[4, pieces[n], side]
        return copy(at, part, part, twin)

    def pump(hop, which):
        for n in which:
            (to_vis(n) if hop == 1 else to_z(hop - 1, n)).wait_recv()
            if hop < 4:
                started.append(to_z(hop, n))
                started[-1].start()
            started.append(to_mate(hop, n))
            started[-1].start()

    def keep_half(rows):
        for q in range(2):
            parts = [own[rows, p * QUARTER : (p + 1) * QUARTER] for p in (2 * q, 2 * q + 1)]
            picked = jnp.where(c == 0, parts[0].astype(F32), parts[1].astype(F32)).astype(BF16)
            half_own[rows, q * QUARTER : (q + 1) * QUARTER] = picked
        held[rows, lanes(x)] = half_own[rows, :]

    @pl.when(y_hi == 1)
    def _():
        for n in vectors:
            to_base(n).start()

    for n in vectors:
        started.append(to_vis(n))
        started[-1].start()
    keep_half(pairs)
    pair_x = {}
    feat_x = {}

    def send_pair(k):
        part = held.at[pairs, lanes(x)]
        pair_x[k] = send(15 + k, part, part, x_peers[k - 1])

    def send_feat(k):
        part = held.at[feats, lanes(x)]
        feat_x[k] = send(19 + k, part, part, x_peers[k - 1])

    send_pair(1)
    send_pair(3)
    send_pair(2)
    for i in range(1, 4):
        features(i)
    scale_row_v = scale_row[...]
    eye = lax.broadcasted_iota(jnp.int32, (FEAT, FEAT), 0) == lax.broadcasted_iota(jnp.int32, (FEAT, FEAT), 1)
    scale = jnp.sum(jnp.where(eye, scale_row_v, 0.0), axis=1, keepdims=True)
    scaled = (dot(w_t[...], hidden[...], 1, 1) * scale).astype(BF16)
    own[feats, :] = scaled
    @pl.when(y_hi == 1)
    def _():
        to_base(2).start()

    started.append(to_vis(2))
    started[-1].start()
    keep_half(feats)
    send_feat(1)
    send_feat(3)
    send_feat(2)

    @pl.when(y_hi == 0)
    def _():
        vis[0] = own[...]

    def ready(index):
        y = held[feats, lanes(index)]
        left[feats, lanes(index)] = y
        left[FEAT:AUG, lanes(index)] = norm_rows(y, False)
        left[AUG:128, lanes(index)] = jnp.zeros((128 - AUG, HALF), BF16)

    def derive(block, at):
        span = slice(at, at + TOK)
        y = block[feats, :]
        augmented = jnp.concatenate([y, norm_rows(y, True)], axis=0)
        vis_b[:, span] = augmented
        padded = jnp.concatenate([augmented, jnp.zeros((128 - AUG, TOK), BF16)], axis=0)
        vis_y[span, :] = padded.T
        swapped = jnp.concatenate([block[2 * FEAT : MSG, :], block[FEAT : 2 * FEAT, :]], axis=0)
        vis_q[span, :] = swapped.T

    def couple(i, at, size):
        span = slice(at, at + size)
        exponent = dot(vis_y[span, :], left[:, i], 1, 0)
        coupling = dot(vis_q[span, :], held[pairs, i], 1, 0)
        weight = (coupling * jnp.exp(exponent)).astype(BF16)
        return dot(vis_b[:, span], weight, 1, 0)

    def meet(k):
        feat_x[k].wait_recv()
        pair_x[k].wait_recv()
        index = lax.rem(x + NX - k, NX)
        ready(index)
        acc[:, lanes(index)] = couple(lanes(index), 0, TOK)

    def visit(block):
        derive(block, 0)
        acc[...] += couple(slice(None), 0, TOK)

    def arrived(hop):
        for n in everything:
            to_mate(hop, n).wait_recv()

    ready(x)

    @pl.when(y_hi == 1)
    def _():
        for n in everything:
            to_base(n).wait_recv()
            share_base(n).start()
        for n in everything:
            share_base(n).wait_recv()

    derive(vis.at[0], 0)
    acc[:, lanes(x)] = couple(lanes(x), 0, TOK)
    slab_t[...] = points[:, aligned(rep * 256, 256, 256)].T
    h32 = hidden[...].astype(F32)
    slope[...] = 1.0 - h32 * h32
    pump(1, vectors)
    meet(1)
    pump(1, (2,))
    meet(3)
    meet(2)
    visit(vis.at[1])
    pump(2, vectors)
    arrived(1)
    visit(mate.at[0])
    pump(2, (2,))
    visit(vis.at[2])
    pump(3, vectors)
    arrived(2)
    visit(mate.at[1])
    pump(3, (2,))
    visit(vis.at[3])
    pump(4, everything)
    arrived(3)
    derive(mate.at[2], 0)
    arrived(4)
    derive(vis.at[4], TOK)

    parts = []

    def finish(k):
        index = lax.rem(x + k, NX)
        i = lanes(index)
        pull = acc[:, i] + couple(i, 0, 2 * TOK)
        drift = pull[feats] - held[feats, i].astype(F32) * pull[FEAT : FEAT + 1]
        part_out[k] = drift.astype(BF16)
        parts.append(send(41 + k, part_out.at[k], part_in.at[4 + k], device(index, z, y_lo, 1 - y_hi, c)))
        if k:
            parts.append(send(37 + k, part_out.at[k], part_in.at[k], device(index, z, y_lo, y_hi, c)))
        return drift

    finish(2)
    finish(1)
    finish(3)
    total = finish(0)
    for one in parts:
        one.wait_recv()
    for k in range(1, 8):
        total = total + part_in[k].astype(F32)
    total = total * scale
    feat_out[...] = jnp.where(y_hi == 0, total[:, 0:QUARTER], total[:, QUARTER:HALF])
    halves[c] = total.astype(BF16)
    send(86, halves.at[c], halves.at[c], twin).wait_recv()
    for q in range(4):
        at = (q // 2) * QUARTER
        grad[:, q * QUARTER : (q + 1) * QUARTER] = halves[q % 2, :, at : at + QUARTER]

    norm = 1.0 / math.sqrt(NPTS)
    pre = dot(grad[...], w_t[...], 0, 0) * slope[...]
    gw = dot(slab_t[...], pre.astype(BF16), 1, 0) * norm
    bias = jnp.sum(pre, axis=0, keepdims=True) * norm
    gwo = dot(grad[aligned(rep * 16, 16, 16), :], hidden[...], 1, 0) * norm
    msg[0, 0:128, :] = gw[0:128].astype(BF16)
    msg[1, 0:128, :] = gw[128:256].astype(BF16)
    msg[0, 128:144, :] = gwo.astype(BF16)
    msg[1, 128:144, :] = jnp.broadcast_to(bias, (16, HID)).astype(BF16)

    def strip(px):
        return aligned(px * 128, 128, 128)

    cell = y_lo * NX + x
    plane = []
    column = []
    for d in range(1, 8):
        other = lax.rem(cell + d, 8)
        plane.append((lax.rem(other, NX), lax.div(other, NX)))
        column.append(lax.rem(z + d, NZ))
    arrivals = []
    for d in range(1, 8):
        px, py = plane[d - 1]
        arrivals.append(send(44 + d, msg.at[py, :, strip(px)], recv_a.at[d - 1], device(px, z, py, y_hi, c)))
    summed = msg[y_lo, :, strip(x)].astype(F32)
    for d in range(1, 8):
        arrivals[d - 1].wait_recv()
        summed = summed + recv_a[d - 1].astype(F32)
    summed_b = summed.astype(BF16)
    for b in range(NZ):
        stage_b[b, 0:16, :] = summed_b[b * 16 : b * 16 + 16]
        stage_b[b, 16:32, :] = summed_b[128:144]
    arrivals = []
    for d in (4, 3, 5, 2, 6, 1, 7):
        pz = column[d - 1]
        arrivals.append(send(51 + d, stage_b.at[pz], recv_b.at[d - 1], device(x, pz, y_lo, y_hi, c)))
    for one in arrivals:
        one.wait_recv()
    tile = stage_b[z].astype(F32)
    for d in range(1, 8):
        tile = tile + recv_b[d - 1].astype(F32)
    tile_b = tile.astype(BF16)
    band = aligned(z * 16, 16, 16)
    chunk[band, :] = tile_b[0:16]
    chunk[128:144, :] = tile_b[16:32]
    arrivals = []
    for d in (4, 3, 5, 2, 6, 1, 7):
        pz = column[d - 1]
        arrivals.append(send(58 + d, chunk.at[band], chunk.at[band], device(x, pz, y_lo, y_hi, c)))
    for one in arrivals:
        one.wait_recv()
    place_mine = table.at[y_hi, c, y_lo, :, strip(x)]
    groups = []
    for dh in range(2):
        for dl in range(2):
            hi = y_hi + dh - 2 * y_hi * dh
            lo = y_lo + dl - 2 * y_lo * dl
            groups.append((dh, dl, hi, lo, []))
    for dx in (2, 1, 3, 0):
        for dh, dl, hi, lo, got in groups[::-1]:
            if dh or dl or dx:
                at = 65 + dh * 8 + dl * 4 + dx
                peer = device(lax.rem(x + dx, NX), z, lo, hi, c)
                got.append(send(at, chunk, place_mine, peer))
    table[y_hi, c, y_lo, :, strip(x)] = chunk[...]
    shared = []
    stores = []

    def store(at, h, core, half):
        row = (h * 2 + core) * 256 + half * 128
        one = pltpu.make_async_copy(table.at[h, core, half, 0:128, :], w_in_out.at[aligned(row, 128, 128), :], out_sem.at[at])
        one.start()
        stores.append(one)

    for n, (dh, dl, hi, lo, got) in enumerate(groups):
        for one in got:
            one.wait_recv()
        part = table.at[hi, c, lo]
        shared.append(send(82 + n, part, part, twin))
        store(n, hi, c, lo)
    for n, (dh, dl, hi, lo, got) in enumerate(groups):
        shared[n].wait_recv()
        store(4 + n, hi, 1 - c, lo)
    b_in_out[...] = table[0, 0, 1, 128:144, :].astype(F32)[0:1]
    for q in range(4):
        w_out_out[q * 16 : q * 16 + 16, :] = table[q // 2, q % 2, 0, 128:144, :].astype(F32)
    for one in started:
        one.wait_send()
    for one in stores:
        one.wait()

    @pl.when(y_hi == 1)
    def _():
        for n in everything:
            to_base(n).wait_send()
            share_base(n).wait_send()


def write_kernel(feat, w_in, b_in, w_out, feat_out, w_in_out, b_in_out, w_out_out):
    feat_out[...] = feat[...]
    w_in_out[...] = w_in[...].astype(F32)
    b_in_out[...] = b_in[...]
    w_out_out[...] = w_out[...]


def write(feat, w_in, b_in, w_out):
    specs = []
    for part in (feat, w_in, b_in, w_out):
        if part is w_in:
            specs.append(pl.BlockSpec((DIN // 4, HID), lambda i: (i, 0)))
        else:
            specs.append(pl.BlockSpec(part.shape, lambda i: (0, 0)))
    return pl.pallas_call(
        write_kernel,
        grid=(4,),
        out_shape=tuple(jax.ShapeDtypeStruct(part.shape, F32) for part in (feat, w_in, b_in, w_out)),
        in_specs=specs,
        out_specs=tuple(specs),
        name="write",
    )(feat, w_in, b_in, w_out)


def on_device(points, w_in, b_in, w_out, inv_scale, solves, probes):
    vmem = pl.BlockSpec(memory_space=pltpu.VMEM)
    hbm = pl.BlockSpec(memory_space=pl.ANY)
    parts = pl.pallas_call(
        kernel,
        out_shape=(
            jax.ShapeDtypeStruct((FEAT, QUARTER), F32),
            jax.ShapeDtypeStruct((DIN, HID), BF16),
            jax.ShapeDtypeStruct((1, HID), F32),
            jax.ShapeDtypeStruct((FEAT, HID), F32),
        ),
        in_specs=[hbm, hbm, vmem, vmem, vmem, hbm, hbm],
        out_specs=(vmem, hbm, vmem, vmem),
        scratch_shapes=[
            pltpu.VMEM((TOK, DIN), BF16),
            pltpu.VMEM((DIN, HID), BF16),
            pltpu.VMEM((TOK, HID), BF16),
            pltpu.VMEM((TOK, HID), F32),
            pltpu.VMEM((256, TOK), BF16),
            pltpu.VMEM((MSG, TOK), BF16),
            pltpu.VMEM((MSG, NX * HALF), BF16),
            pltpu.VMEM((5, MSG, TOK), BF16),
            pltpu.VMEM((3, MSG, TOK), BF16),
            pltpu.VMEM((128, NX * HALF), BF16),
            pltpu.VMEM((AUG, 2 * TOK), BF16),
            pltpu.VMEM((2 * TOK, 128), BF16),
            pltpu.VMEM((2 * TOK, 128), BF16),
            pltpu.VMEM((AUG, NX * HALF), F32),
            pltpu.VMEM((MSG, HALF), BF16),
            pltpu.VMEM((4, FEAT, HALF), BF16),
            pltpu.VMEM((8, FEAT, HALF), BF16),
            pltpu.VMEM((2, FEAT, HALF), BF16),
            pltpu.VMEM((FEAT, TOK), BF16),
            pltpu.VMEM((2, ROWS, HID), BF16),
            pltpu.VMEM((7, ROWS, 128), BF16),
            pltpu.VMEM((NZ, 32, 128), BF16),
            pltpu.VMEM((7, 32, 128), BF16),
            pltpu.VMEM((ROWS, 128), BF16),
            pltpu.VMEM((2, 2, 2, ROWS, HID), BF16),
            pltpu.SemaphoreType.DMA((7,)),
            pltpu.SemaphoreType.DMA((87,)),
            pltpu.SemaphoreType.DMA((87,)),
            pltpu.SemaphoreType.DMA((8,)),
        ],
        compiler_params=pltpu.CompilerParams(
            collective_id=1, has_side_effects=True, vmem_limit_bytes=56 << 20
        ),
        name="trace_term",
    )(points, w_in, b_in[None, :], w_out.T, inv_scale[None, :], solves, probes)
    feat_grad, grad_w_in, grad_b_in, grad_w_out = write(*parts)
    return feat_grad, grad_w_in, grad_b_in[0], grad_w_out.T


def solution(mesh):
    in_specs = (P("blk", None), P(), P(), P(), P(), P(None, "blk"), P(None, "blk"))
    out_specs = (P(None, ("blk", "rep")), P(), P(), P())
    return jax.shard_map(
        on_device, mesh=mesh, in_specs=in_specs, out_specs=out_specs, check_vma=False
    )
```

```python
import math

import jax
import jax.numpy as jnp
from jax import lax
from jax.experimental import pallas as pl
from jax.experimental.pallas import tpu as pltpu
from jax.sharding import PartitionSpec as P

MESH = pl.DeviceIdType.MESH
F32 = jnp.float32
BF16 = jnp.bfloat16
DIN, HID, FEAT, TOK, QUARTER = 1024, 512, 64, 768, 192
HALF = TOK // 2
NX, NZ = 4, 8
ROWS = 144
MSG = 192
AUG = 80
NPTS = 49152


def dot(a, b, ca, cb):
    return lax.dot_general(a, b, (((ca,), (cb,)), ((), ())), preferred_element_type=F32)


def place():
    blk = lax.axis_index("blk")
    rep = lax.axis_index("rep")
    x = lax.rem(blk, NX)
    z = lax.rem(lax.div(blk, NX), NZ)
    y_lo = lax.div(blk, NX * NZ)
    return x, z, y_lo, lax.div(rep, 2), lax.rem(rep, 2)


def device(x, z, y_lo, y_hi, c):
    return ((y_lo * NZ + z) * NX + x, y_hi * 2 + c)


def aligned(start, size, step):
    return pl.ds(pl.multiple_of(start, step), size)


def norm_rows(y, ones_first):
    y32 = y.astype(F32)
    half_sq = -0.5 * jnp.sum(y32 * y32, axis=0, keepdims=True)
    high = half_sq.astype(BF16).astype(F32)
    mid = (half_sq - high).astype(BF16).astype(F32)
    low = (half_sq - high - mid).astype(BF16).astype(F32)
    row = lax.broadcasted_iota(jnp.int32, (16, y.shape[1]), 0)
    base = 3 if ones_first else 0
    ones = 0 if ones_first else 3
    rows = jnp.where((row >= ones) & (row < ones + 3), 1.0, 0.0)
    rows = jnp.where(row == base, high, rows)
    rows = jnp.where(row == base + 1, mid, rows)
    rows = jnp.where(row == base + 2, low, rows)
    return rows.astype(BF16)


def kernel(
    points_in, w_in_any, b_in, w_t, scale_row, solves, probes,
    feat_out, w_in_out, b_in_out, w_out_out,
    points, w_in, hidden, slope, slab_t, own, held, vis, mate, left, vis_b, vis_y, vis_q, acc,
    half_own, part_out, part_in, halves, grad, msg, recv_a, stage_b, recv_b, chunk, table,
    load_sem, send_sem, recv_sem, out_sem,
):
    x, z, y_lo, y_hi, c = place()
    rep = y_hi * 2 + c
    step = 1 - 2 * c
    y_vis = y_lo + y_hi - 2 * y_lo * y_hi
    x_next = lax.rem(x + step + NX, NX)
    x_prev = lax.rem(x - step + NX, NX)
    x_far = lax.rem(x + 2, NX)
    z_next = lax.rem(z + step + NZ, NZ)
    z_prev = lax.rem(z - step + NZ, NZ)
    twin = device(x, z, y_lo, y_hi, 1 - c)
    next_z = device(x, z_next, y_lo, y_hi, c)
    near = [device(one, z, y_lo, y_hi, c) for one in (x_next, x_prev, x_far)]
    near += [device(x, one, y_lo, y_hi, c) for one in (z_next, z_prev)]
    near += [device(x, one, 1 - y_lo, y_hi, c) for one in (z, z_next, z_prev)]
    near += [twin, device(x, z, y_lo, 1 - y_hi, c)]

    def lanes(index):
        return aligned(index * HALF, HALF, HALF)

    started = []

    def copy(at, src, dst, peer):
        return pltpu.make_async_remote_copy(
            src_ref=src,
            dst_ref=dst,
            send_sem=send_sem.at[at],
            recv_sem=recv_sem.at[at],
            device_id=peer,
            device_id_type=MESH,
        )

    def send(at, src, dst, peer):
        one = copy(at, src, dst, peer)
        one.start()
        started.append(one)
        return one

    def load(at, src, dst):
        return pltpu.make_async_copy(src, dst, load_sem.at[at])

    barrier = pltpu.get_barrier_semaphore()
    for peer in near:
        pl.semaphore_signal(barrier, inc=1, device_id=peer, device_id_type=MESH)
    loads = [
        load(0, solves, own.at[FEAT : 2 * FEAT]),
        load(1, probes, own.at[2 * FEAT : MSG]),
        load(2, w_in_any, w_in),
    ]
    for i in range(2):
        part = slice(i * HALF, (i + 1) * HALF)
        loads.append(load(3 + i, points_in.at[part], points.at[part]))
    for one in loads:
        one.start()

    def features(i):
        part = slice(i * HALF, (i + 1) * HALF)
        loads[3 + i].wait()
        pre = dot(points[part], w_in[...], 1, 0) + b_in[...]
        hidden[part] = jnp.tanh(pre).astype(BF16)

    for one in loads[:3]:
        one.wait()
    features(0)
    pl.semaphore_wait(barrier, len(near))

    pairs = slice(FEAT, MSG)
    feats = slice(0, FEAT)
    pieces = [slice(FEAT, 2 * FEAT), slice(2 * FEAT, MSG), feats]
    vectors = (0, 1)
    everything = (0, 1, 2)
    side = aligned(c * HALF, HALF, HALF)
    x_peers = [device(lax.rem(x + k, NX), z, y_lo, y_hi, c) for k in range(1, 4)]
    visited = device(x, z_next, y_vis, y_hi, c)

    def to_vis(n):
        return copy(n, own.at[pieces[n]], vis.at[1, pieces[n]], visited)

    def to_base(n):
        return copy(3 + n, own.at[pieces[n], side], vis.at[0, pieces[n], side], device(x, z, 1 - y_lo, y_hi, c))

    def share_base(n):
        part = vis.at[0, pieces[n], side]
        return copy(35 + n, part, part, twin)

    def to_z(hop, n):
        at = 6 + 3 * (hop - 1) + n
        if hop < 3:
            return copy(at, vis.at[hop, pieces[n]], vis.at[hop + 1, pieces[n]], next_z)
        return copy(at, vis.at[3, pieces[n], side], vis.at[4, pieces[n], side], next_z)

    def to_mate(hop, n):
        at = 23 + 3 * (hop - 1) + n
        if hop < 4:
            return copy(at, vis.at[hop, pieces[n]], mate.at[hop - 1, pieces[n]], twin)
        part = vis.at[4, pieces[n], side]
        return copy(at, part, part, twin)

    def pump(hop, which):
        for n in which:
            (to_vis(n) if hop == 1 else to_z(hop - 1, n)).wait_recv()
            if hop < 4:
                started.append(to_z(hop, n))
                started[-1].start()
            started.append(to_mate(hop, n))
            started[-1].start()

    def keep_half(rows):
        for q in range(2):
            parts = [own[rows, p * QUARTER : (p + 1) * QUARTER] for p in (2 * q, 2 * q + 1)]
            picked = jnp.where(c == 0, parts[0].astype(F32), parts[1].astype(F32)).astype(BF16)
            half_own[rows, q * QUARTER : (q + 1) * QUARTER] = picked
        held[rows, lanes(x)] = half_own[rows, :]

    @pl.when(y_hi == 1)
    def _():
        for n in vectors:
            to_base(n).start()

    for n in vectors:
        started.append(to_vis(n))
        started[-1].start()
    keep_half(pairs)
    pair_x = {}
    feat_x = {}

    def send_pair(k):
        part = held.at[pairs, lanes(x)]
        pair_x[k] = send(15 + k, part, part, x_peers[k - 1])

    def send_feat(k):
        part = held.at[feats, lanes(x)]
        feat_x[k] = send(19 + k, part, part, x_peers[k - 1])

    send_pair(1)
    send_pair(3)
    send_pair(2)
    features(1)
    scale_row_v = scale_row[...]
    eye = lax.broadcasted_iota(jnp.int32, (FEAT, FEAT), 0) == lax.broadcasted_iota(jnp.int32, (FEAT, FEAT), 1)
    scale = jnp.sum(jnp.where(eye, scale_row_v, 0.0), axis=1, keepdims=True)
    scaled = (dot(w_t[...], hidden[...], 1, 1) * scale).astype(BF16)
    own[feats, :] = scaled
    @pl.when(y_hi == 1)
    def _():
        to_base(2).start()

    started.append(to_vis(2))
    started[-1].start()
    keep_half(feats)
    send_feat(1)
    send_feat(3)
    send_feat(2)

    @pl.when(y_hi == 0)
    def _():
        vis[0] = own[...]

    def ready(index):
        y = held[feats, lanes(index)]
        left[feats, lanes(index)] = y
        left[FEAT:AUG, lanes(index)] = norm_rows(y, False)
        left[AUG:128, lanes(index)] = jnp.zeros((128 - AUG, HALF), BF16)

    def derive(block, at):
        span = slice(at, at + TOK)
        y = block[feats, :]
        augmented = jnp.concatenate([y, norm_rows(y, True)], axis=0)
        vis_b[:, span] = augmented
        padded = jnp.concatenate([augmented, jnp.zeros((128 - AUG, TOK), BF16)], axis=0)
        vis_y[span, :] = padded.T
        swapped = jnp.concatenate([block[2 * FEAT : MSG, :], block[FEAT : 2 * FEAT, :]], axis=0)
        vis_q[span, :] = swapped.T

    def couple(i, at, size):
        span = slice(at, at + size)
        exponent = dot(vis_y[span, :], left[:, i], 1, 0)
        coupling = dot(vis_q[span, :], held[pairs, i], 1, 0)
        weight = (coupling * jnp.exp(exponent)).astype(BF16)
        return dot(vis_b[:, span], weight, 1, 0)

    def meet(k):
        feat_x[k].wait_recv()
        pair_x[k].wait_recv()
        index = lax.rem(x + NX - k, NX)
        ready(index)
        acc[:, lanes(index)] = couple(lanes(index), 0, TOK)

    def visit(block):
        derive(block, 0)
        acc[...] += couple(slice(None), 0, TOK)

    def arrived(hop):
        for n in everything:
            to_mate(hop, n).wait_recv()

    ready(x)

    @pl.when(y_hi == 1)
    def _():
        for n in everything:
            to_base(n).wait_recv()
            share_base(n).start()
        for n in everything:
            share_base(n).wait_recv()

    derive(vis.at[0], 0)
    acc[:, lanes(x)] = couple(lanes(x), 0, TOK)
    slab_t[...] = points[:, aligned(rep * 256, 256, 256)].T
    h32 = hidden[...].astype(F32)
    slope[...] = 1.0 - h32 * h32
    meet(1)
    pump(1, vectors)
    meet(3)
    pump(1, (2,))
    meet(2)
    visit(vis.at[1])
    pump(2, vectors)
    arrived(1)
    visit(mate.at[0])
    pump(2, (2,))
    visit(vis.at[2])
    pump(3, vectors)
    arrived(2)
    visit(mate.at[1])
    pump(3, (2,))
    visit(vis.at[3])
    pump(4, everything)
    arrived(3)
    derive(mate.at[2], 0)
    arrived(4)
    derive(vis.at[4], TOK)

    parts = []

    def finish(k):
        index = lax.rem(x + k, NX)
        i = lanes(index)
        pull = acc[:, i] + couple(i, 0, 2 * TOK)
        drift = pull[feats] - held[feats, i].astype(F32) * pull[FEAT : FEAT + 1]
        part_out[k] = drift.astype(BF16)
        parts.append(send(41 + k, part_out.at[k], part_in.at[4 + k], device(index, z, y_lo, 1 - y_hi, c)))
        if k:
            parts.append(send(37 + k, part_out.at[k], part_in.at[k], device(index, z, y_lo, y_hi, c)))
        return drift

    finish(2)
    finish(1)
    finish(3)
    total = finish(0)
    for one in parts:
        one.wait_recv()
    for k in range(1, 8):
        total = total + part_in[k].astype(F32)
    total = total * scale
    feat_out[...] = jnp.where(y_hi == 0, total[:, 0:QUARTER], total[:, QUARTER:HALF])
    halves[c] = total.astype(BF16)
    send(86, halves.at[c], halves.at[c], twin).wait_recv()
    for q in range(4):
        at = (q // 2) * QUARTER
        grad[:, q * QUARTER : (q + 1) * QUARTER] = halves[q % 2, :, at : at + QUARTER]

    norm = 1.0 / math.sqrt(NPTS)
    pre = dot(grad[...], w_t[...], 0, 0) * slope[...]
    pre_b = pre.astype(BF16)
    def strip(px):
        return aligned(px * 128, 128, 128)

    column = []
    for d in range(1, 8):
        column.append(lax.rem(z + d, NZ))
    arrivals = []

    def scatter(row, first):
        msg[row, 0:128, :] = (dot(slab_t[aligned(row * 128, 128, 128), :], pre_b, 1, 0) * norm).astype(BF16)
        small = jnp.where(row == 0, gwo, bias)
        msg[row, 128:144, :] = small.astype(BF16)
        for dx in (2, 1, 3) if first is None else (2, 1, 3, 0):
            px = lax.rem(x + dx, NX)
            at = (first or 0) + dx
            arrivals.append(send(45 + at, msg.at[row, :, strip(px)], recv_a.at[at], device(px, z, row, y_hi, c)))

    gwo = dot(grad[aligned(rep * 16, 16, 16), :], hidden[...], 1, 0) * norm
    bias = jnp.broadcast_to(jnp.sum(pre, axis=0, keepdims=True) * norm, (16, HID))
    scatter(1 - y_lo, 4)
    scatter(y_lo, None)
    summed = msg[y_lo, :, strip(x)].astype(F32)
    for one in arrivals:
        one.wait_recv()
    for at in range(1, 8):
        summed = summed + recv_a[at].astype(F32)
    summed_b = summed.astype(BF16)
    for b in range(NZ):
        stage_b[b, 0:16, :] = summed_b[b * 16 : b * 16 + 16]
        stage_b[b, 16:32, :] = summed_b[128:144]
    arrivals = []
    for d in (4, 3, 5, 2, 6, 1, 7):
        pz = column[d - 1]
        arrivals.append(send(87 + d, stage_b.at[pz], recv_b.at[d - 1], device(x, pz, y_lo, y_hi, c)))
    for one in arrivals:
        one.wait_recv()
    tile = stage_b[z].astype(F32)
    for d in range(1, 8):
        tile = tile + recv_b[d - 1].astype(F32)
    tile_b = tile.astype(BF16)
    band = aligned(z * 16, 16, 16)
    chunk[band, :] = tile_b[0:16]
    chunk[128:144, :] = tile_b[16:32]
    arrivals = []
    for d in (4, 3, 5, 2, 6, 1, 7):
        pz = column[d - 1]
        arrivals.append(send(58 + d, chunk.at[band], chunk.at[band], device(x, pz, y_lo, y_hi, c)))
    for one in arrivals:
        one.wait_recv()
    place_mine = table.at[y_hi, c, y_lo, :, strip(x)]
    groups = []
    for dh in range(2):
        for dl in range(2):
            hi = y_hi + dh - 2 * y_hi * dh
            lo = y_lo + dl - 2 * y_lo * dl
            groups.append((dh, dl, hi, lo, []))
    for dx in (2, 1, 3, 0):
        for dh, dl, hi, lo, got in groups[::-1]:
            if dh or dl or dx:
                at = 65 + dh * 8 + dl * 4 + dx
                peer = device(lax.rem(x + dx, NX), z, lo, hi, c)
                got.append(send(at, chunk, place_mine, peer))
    table[y_hi, c, y_lo, :, strip(x)] = chunk[...]
    shared = []
    stores = []

    def store(at, h, core, half):
        row = (h * 2 + core) * 256 + half * 128
        one = pltpu.make_async_copy(table.at[h, core, half, 0:128, :], w_in_out.at[aligned(row, 128, 128), :], out_sem.at[at])
        one.start()
        stores.append(one)

    for n, (dh, dl, hi, lo, got) in enumerate(groups):
        for one in got:
            one.wait_recv()
        part = table.at[hi, c, lo]
        shared.append(send(82 + n, part, part, twin))
        store(n, hi, c, lo)
    for n, (dh, dl, hi, lo, got) in enumerate(groups):
        shared[n].wait_recv()
        store(4 + n, hi, 1 - c, lo)
    b_in_out[...] = table[0, 0, 1, 128:144, :].astype(F32)[0:1]
    for q in range(4):
        w_out_out[q * 16 : q * 16 + 16, :] = table[q // 2, q % 2, 0, 128:144, :].astype(F32)
    for one in started:
        one.wait_send()
    for one in stores:
        one.wait()

    @pl.when(y_hi == 1)
    def _():
        for n in everything:
            to_base(n).wait_send()
            share_base(n).wait_send()


def write_kernel(feat, w_in, b_in, w_out, feat_out, w_in_out, b_in_out, w_out_out, narrow, wide, load_sem, store_sem):
    count = 8
    rows = [slice(i * DIN // count, (i + 1) * DIN // count) for i in range(count)]
    loads = [pltpu.make_async_copy(w_in.at[r], narrow.at[r], load_sem.at[i]) for i, r in enumerate(rows)]
    stores = [pltpu.make_async_copy(wide.at[r], w_in_out.at[r], store_sem.at[i]) for i, r in enumerate(rows)]
    for one in loads:
        one.start()
    pairs = ((feat, feat_out), (b_in, b_in_out), (w_out, w_out_out))
    small = [pltpu.make_async_copy(src, dst, store_sem.at[count + i]) for i, (src, dst) in enumerate(pairs)]
    for one in small:
        one.start()
    for i, r in enumerate(rows):
        loads[i].wait()
        wide[r] = narrow[r].astype(F32)
        stores[i].start()
    for one in small + stores:
        one.wait()


def write(feat, w_in, b_in, w_out):
    free = pl.BlockSpec(memory_space=pl.ANY)
    return pl.pallas_call(
        write_kernel,
        out_shape=tuple(jax.ShapeDtypeStruct(part.shape, F32) for part in (feat, w_in, b_in, w_out)),
        in_specs=[free] * 4,
        out_specs=(free,) * 4,
        scratch_shapes=[
            pltpu.VMEM((DIN, HID), BF16),
            pltpu.VMEM((DIN, HID), F32),
            pltpu.SemaphoreType.DMA((8,)),
            pltpu.SemaphoreType.DMA((11,)),
        ],
        compiler_params=pltpu.CompilerParams(vmem_limit_bytes=56 << 20),
        name="write",
    )(feat, w_in, b_in, w_out)


def on_device(points, w_in, b_in, w_out, inv_scale, solves, probes):
    vmem = pl.BlockSpec(memory_space=pltpu.VMEM)
    hbm = pl.BlockSpec(memory_space=pltpu.HBM)
    free = pl.BlockSpec(memory_space=pl.ANY)
    parts = pl.pallas_call(
        kernel,
        out_shape=(
            jax.ShapeDtypeStruct((FEAT, QUARTER), F32),
            jax.ShapeDtypeStruct((DIN, HID), BF16),
            jax.ShapeDtypeStruct((1, HID), F32),
            jax.ShapeDtypeStruct((FEAT, HID), F32),
        ),
        in_specs=[hbm, hbm, vmem, vmem, vmem, hbm, hbm],
        out_specs=(vmem, free, vmem, vmem),
        scratch_shapes=[
            pltpu.VMEM((TOK, DIN), BF16),
            pltpu.VMEM((DIN, HID), BF16),
            pltpu.VMEM((TOK, HID), BF16),
            pltpu.VMEM((TOK, HID), F32),
            pltpu.VMEM((256, TOK), BF16),
            pltpu.VMEM((MSG, TOK), BF16),
            pltpu.VMEM((MSG, NX * HALF), BF16),
            pltpu.VMEM((5, MSG, TOK), BF16),
            pltpu.VMEM((3, MSG, TOK), BF16),
            pltpu.VMEM((128, NX * HALF), BF16),
            pltpu.VMEM((AUG, 2 * TOK), BF16),
            pltpu.VMEM((2 * TOK, 128), BF16),
            pltpu.VMEM((2 * TOK, 128), BF16),
            pltpu.VMEM((AUG, NX * HALF), F32),
            pltpu.VMEM((MSG, HALF), BF16),
            pltpu.VMEM((4, FEAT, HALF), BF16),
            pltpu.VMEM((8, FEAT, HALF), BF16),
            pltpu.VMEM((2, FEAT, HALF), BF16),
            pltpu.VMEM((FEAT, TOK), BF16),
            pltpu.VMEM((2, ROWS, HID), BF16),
            pltpu.VMEM((8, ROWS, 128), BF16),
            pltpu.VMEM((NZ, 32, 128), BF16),
            pltpu.VMEM((7, 32, 128), BF16),
            pltpu.VMEM((ROWS, 128), BF16),
            pltpu.VMEM((2, 2, 2, ROWS, HID), BF16),
            pltpu.SemaphoreType.DMA((7,)),
            pltpu.SemaphoreType.DMA((95,)),
            pltpu.SemaphoreType.DMA((95,)),
            pltpu.SemaphoreType.DMA((8,)),
        ],
        compiler_params=pltpu.CompilerParams(
            collective_id=1, has_side_effects=True, vmem_limit_bytes=56 << 20
        ),
        name="trace_term",
    )(points, w_in, b_in[None, :], w_out.T, inv_scale[None, :], solves, probes)
    feat_grad, grad_w_in, grad_b_in, grad_w_out = write(*parts)
    return feat_grad, grad_w_in, grad_b_in[0], grad_w_out.T


def solution(mesh):
    in_specs = (P("blk", None), P(), P(), P(), P(), P(None, "blk"), P(None, "blk"))
    out_specs = (P(None, ("blk", "rep")), P(), P(), P())
    return jax.shard_map(
        on_device, mesh=mesh, in_specs=in_specs, out_specs=out_specs, check_vma=False
    )
```

```python
import math

import jax
import jax.numpy as jnp
from jax import lax
from jax.experimental import pallas as pl
from jax.experimental.pallas import tpu as pltpu
from jax.sharding import PartitionSpec as P

MESH = pl.DeviceIdType.MESH
F32 = jnp.float32
BF16 = jnp.bfloat16
DIN, HID, FEAT, TOK, QUARTER = 1024, 512, 64, 768, 192
HALF = TOK // 2
NX, NZ = 4, 8
ROWS = 144
MSG = 192
AUG = 80
NPTS = 49152


def dot(a, b, ca, cb):
    return lax.dot_general(a, b, (((ca,), (cb,)), ((), ())), preferred_element_type=F32)


def place():
    blk = lax.axis_index("blk")
    rep = lax.axis_index("rep")
    x = lax.rem(blk, NX)
    z = lax.rem(lax.div(blk, NX), NZ)
    y_lo = lax.div(blk, NX * NZ)
    return x, z, y_lo, lax.div(rep, 2), lax.rem(rep, 2)


def device(x, z, y_lo, y_hi, c):
    return ((y_lo * NZ + z) * NX + x, y_hi * 2 + c)


def aligned(start, size, step):
    return pl.ds(pl.multiple_of(start, step), size)


def norm_rows(y, ones_first):
    y32 = y.astype(F32)
    half_sq = -0.5 * jnp.sum(y32 * y32, axis=0, keepdims=True)
    high = half_sq.astype(BF16).astype(F32)
    mid = (half_sq - high).astype(BF16).astype(F32)
    low = (half_sq - high - mid).astype(BF16).astype(F32)
    row = lax.broadcasted_iota(jnp.int32, (16, y.shape[1]), 0)
    base = 3 if ones_first else 0
    ones = 0 if ones_first else 3
    rows = jnp.where((row >= ones) & (row < ones + 3), 1.0, 0.0)
    rows = jnp.where(row == base, high, rows)
    rows = jnp.where(row == base + 1, mid, rows)
    rows = jnp.where(row == base + 2, low, rows)
    return rows.astype(BF16)


def kernel(
    points_in, w_in_any, b_in, w_t, scale_row, solves, probes,
    feat_out, w_in_out, b_in_out, w_out_out,
    points, w_in, hidden, slope, slab_t, own, held, vis, mate, left, vis_b, vis_y, vis_q, acc,
    half_own, part_out, part_in, halves, grad, msg, recv_a, stage_b, recv_b, chunk, table,
    load_sem, send_sem, recv_sem, out_sem,
):
    x, z, y_lo, y_hi, c = place()
    rep = y_hi * 2 + c
    step = 1 - 2 * c
    y_vis = y_lo + y_hi - 2 * y_lo * y_hi
    x_next = lax.rem(x + step + NX, NX)
    x_prev = lax.rem(x - step + NX, NX)
    x_far = lax.rem(x + 2, NX)
    z_next = lax.rem(z + step + NZ, NZ)
    z_prev = lax.rem(z - step + NZ, NZ)
    twin = device(x, z, y_lo, y_hi, 1 - c)
    next_z = device(x, z_next, y_lo, y_hi, c)
    near = [device(one, z, y_lo, y_hi, c) for one in (x_next, x_prev, x_far)]
    near += [device(x, one, y_lo, y_hi, c) for one in (z_next, z_prev)]
    near += [device(x, one, 1 - y_lo, y_hi, c) for one in (z, z_next, z_prev)]
    near += [device(x, one, 1 - y_lo, 1 - y_hi, c) for one in (z, z_next, z_prev)]
    near += [twin, device(x, z, y_lo, 1 - y_hi, c)]

    def lanes(index):
        return aligned(index * HALF, HALF, HALF)

    started = []

    def copy(at, src, dst, peer):
        return pltpu.make_async_remote_copy(
            src_ref=src,
            dst_ref=dst,
            send_sem=send_sem.at[at],
            recv_sem=recv_sem.at[at],
            device_id=peer,
            device_id_type=MESH,
        )

    def send(at, src, dst, peer):
        one = copy(at, src, dst, peer)
        one.start()
        started.append(one)
        return one

    def load(at, src, dst):
        return pltpu.make_async_copy(src, dst, load_sem.at[at])

    barrier = pltpu.get_barrier_semaphore()
    for peer in near:
        pl.semaphore_signal(barrier, inc=1, device_id=peer, device_id_type=MESH)
    loads = []
    for i in range(4):
        part = slice(i * QUARTER, (i + 1) * QUARTER)
        loads.append(load(i, points_in.at[part], points.at[part]))
    loads.insert(0, load(6, w_in_any, w_in))
    loads.append(load(4, solves, own.at[FEAT : 2 * FEAT]))
    loads.append(load(5, probes, own.at[2 * FEAT : MSG]))
    for one in loads:
        one.start()

    def features(i):
        part = slice(i * QUARTER, (i + 1) * QUARTER)
        loads[i + 1].wait()
        pre = dot(points[part], w_in[...], 1, 0) + b_in[...]
        hidden[part] = jnp.tanh(pre).astype(BF16)

    loads[5].wait()
    loads[6].wait()
    loads[0].wait()
    features(0)
    pl.semaphore_wait(barrier, len(near))

    pairs = slice(FEAT, MSG)
    feats = slice(0, FEAT)
    pieces = [slice(FEAT, 2 * FEAT), slice(2 * FEAT, MSG), feats]
    vectors = (0, 1)
    everything = (0, 1, 2)
    side = aligned(c * HALF, HALF, HALF)
    x_peers = [device(lax.rem(x + k, NX), z, y_lo, y_hi, c) for k in range(1, 4)]
    visited = device(x, z_next, y_vis, y_hi, c)

    def to_vis(n):
        return copy(n, own.at[pieces[n]], vis.at[1, pieces[n]], visited)

    def to_base(n):
        return copy(3 + n, own.at[pieces[n], side], vis.at[0, pieces[n], side], device(x, z, 1 - y_lo, 1, c))

    def to_cross(n):
        return copy(95 + n, own.at[pieces[n]], vis.at[1, pieces[n]], device(x, z_next, 1 - y_lo, 1, c))

    gives_base = (y_hi + c) == 1
    keeps_chain = (y_hi == 0) | (c == 0)
    gives_cross = (y_hi == 0) & (c == 1)
    takes_cross = (y_hi == 1) & (c == 1)

    def first_sends(which):
        @pl.when(gives_base)
        def _():
            for n in which:
                to_base(n).start()

        @pl.when(keeps_chain)
        def _():
            for n in which:
                to_vis(n).start()

        @pl.when(gives_cross)
        def _():
            for n in which:
                to_cross(n).start()

    def first_arrived(n):
        @pl.when(keeps_chain)
        def _():
            to_vis(n).wait_recv()

        @pl.when(takes_cross)
        def _():
            to_cross(n).wait_recv()

    def share_base(n):
        part = vis.at[0, pieces[n], side]
        return copy(35 + n, part, part, twin)

    def to_z(hop, n):
        at = 6 + 3 * (hop - 1) + n
        if hop < 3:
            return copy(at, vis.at[hop, pieces[n]], vis.at[hop + 1, pieces[n]], next_z)
        return copy(at, vis.at[3, pieces[n], side], vis.at[4, pieces[n], side], next_z)

    def to_mate(hop, n):
        at = 23 + 3 * (hop - 1) + n
        if hop < 4:
            return copy(at, vis.at[hop, pieces[n]], mate.at[hop - 1, pieces[n]], twin)
        part = vis.at[4, pieces[n], side]
        return copy(at, part, part, twin)

    def pump(hop, which):
        for n in which:
            if hop == 1:
                first_arrived(n)
            else:
                to_z(hop - 1, n).wait_recv()
            if hop < 4:
                started.append(to_z(hop, n))
                started[-1].start()
            started.append(to_mate(hop, n))
            started[-1].start()

    def keep_half(rows):
        for q in range(2):
            parts = [own[rows, p * QUARTER : (p + 1) * QUARTER] for p in (2 * q, 2 * q + 1)]
            picked = jnp.where(c == 0, parts[0].astype(F32), parts[1].astype(F32)).astype(BF16)
            half_own[rows, q * QUARTER : (q + 1) * QUARTER] = picked
        held[rows, lanes(x)] = half_own[rows, :]

    first_sends(vectors)
    keep_half(pairs)
    pair_x = {}
    feat_x = {}

    def send_pair(k):
        part = held.at[pairs, lanes(x)]
        pair_x[k] = send(15 + k, part, part, x_peers[k - 1])

    def send_feat(k):
        part = held.at[feats, lanes(x)]
        feat_x[k] = send(19 + k, part, part, x_peers[k - 1])

    send_pair(1)
    send_pair(3)
    send_pair(2)
    for i in range(1, 4):
        features(i)
    scale_row_v = scale_row[...]
    eye = lax.broadcasted_iota(jnp.int32, (FEAT, FEAT), 0) == lax.broadcasted_iota(jnp.int32, (FEAT, FEAT), 1)
    scale = jnp.sum(jnp.where(eye, scale_row_v, 0.0), axis=1, keepdims=True)
    scaled = (dot(w_t[...], hidden[...], 1, 1) * scale).astype(BF16)
    own[feats, :] = scaled
    first_sends((2,))
    keep_half(feats)
    send_feat(1)
    send_feat(3)
    send_feat(2)

    @pl.when(y_hi == 0)
    def _():
        vis[0] = own[...]

    def ready(index):
        y = held[feats, lanes(index)]
        left[feats, lanes(index)] = y
        left[FEAT:AUG, lanes(index)] = norm_rows(y, False)
        left[AUG:128, lanes(index)] = jnp.zeros((128 - AUG, HALF), BF16)

    def derive(block, at):
        span = slice(at, at + TOK)
        y = block[feats, :]
        augmented = jnp.concatenate([y, norm_rows(y, True)], axis=0)
        vis_b[:, span] = augmented
        padded = jnp.concatenate([augmented, jnp.zeros((128 - AUG, TOK), BF16)], axis=0)
        vis_y[span, :] = padded.T
        swapped = jnp.concatenate([block[2 * FEAT : MSG, :], block[FEAT : 2 * FEAT, :]], axis=0)
        vis_q[span, :] = swapped.T

    def couple(i, at, size):
        span = slice(at, at + size)
        exponent = dot(vis_y[span, :], left[:, i], 1, 0)
        coupling = dot(vis_q[span, :], held[pairs, i], 1, 0)
        weight = (coupling * jnp.exp(exponent)).astype(BF16)
        return dot(vis_b[:, span], weight, 1, 0)

    def meet(k):
        feat_x[k].wait_recv()
        pair_x[k].wait_recv()
        index = lax.rem(x + NX - k, NX)
        ready(index)
        acc[:, lanes(index)] = couple(lanes(index), 0, TOK)

    def visit(block):
        derive(block, 0)
        acc[...] += couple(slice(None), 0, TOK)

    def arrived(hop):
        for n in everything:
            to_mate(hop, n).wait_recv()

    ready(x)

    @pl.when(y_hi == 1)
    def _():
        for n in everything:
            to_base(n).wait_recv()
            share_base(n).start()
        for n in everything:
            share_base(n).wait_recv()

    derive(vis.at[0], 0)
    acc[:, lanes(x)] = couple(lanes(x), 0, TOK)
    slab_t[...] = points[:, aligned(rep * 256, 256, 256)].T
    h32 = hidden[...].astype(F32)
    slope[...] = 1.0 - h32 * h32
    pump(1, vectors)
    meet(1)
    pump(1, (2,))
    meet(3)
    meet(2)
    visit(vis.at[1])
    pump(2, vectors)
    arrived(1)
    visit(mate.at[0])
    pump(2, (2,))
    visit(vis.at[2])
    pump(3, vectors)
    arrived(2)
    visit(mate.at[1])
    pump(3, (2,))
    visit(vis.at[3])
    pump(4, everything)
    arrived(3)
    derive(mate.at[2], 0)
    arrived(4)
    derive(vis.at[4], TOK)

    parts = []

    def finish(k):
        index = lax.rem(x + k, NX)
        i = lanes(index)
        pull = acc[:, i] + couple(i, 0, 2 * TOK)
        drift = pull[feats] - held[feats, i].astype(F32) * pull[FEAT : FEAT + 1]
        part_out[k] = drift.astype(BF16)
        parts.append(send(41 + k, part_out.at[k], part_in.at[4 + k], device(index, z, y_lo, 1 - y_hi, c)))
        if k:
            parts.append(send(37 + k, part_out.at[k], part_in.at[k], device(index, z, y_lo, y_hi, c)))
        return drift

    finish(2)
    finish(1)
    finish(3)
    total = finish(0)
    for one in parts:
        one.wait_recv()
    for k in range(1, 8):
        total = total + part_in[k].astype(F32)
    total = total * scale
    feat_out[...] = jnp.where(y_hi == 0, total[:, 0:QUARTER], total[:, QUARTER:HALF])
    halves[c] = total.astype(BF16)
    send(86, halves.at[c], halves.at[c], twin).wait_recv()
    for q in range(4):
        at = (q // 2) * QUARTER
        grad[:, q * QUARTER : (q + 1) * QUARTER] = halves[q % 2, :, at : at + QUARTER]

    norm = 1.0 / math.sqrt(NPTS)
    pre = dot(grad[...], w_t[...], 0, 0) * slope[...]
    gw = dot(slab_t[...], pre.astype(BF16), 1, 0) * norm
    bias = jnp.sum(pre, axis=0, keepdims=True) * norm
    gwo = dot(grad[aligned(rep * 16, 16, 16), :], hidden[...], 1, 0) * norm
    msg[0, 0:128, :] = gw[0:128].astype(BF16)
    msg[1, 0:128, :] = gw[128:256].astype(BF16)
    msg[0, 128:144, :] = gwo.astype(BF16)
    msg[1, 128:144, :] = jnp.broadcast_to(bias, (16, HID)).astype(BF16)

    def strip(px):
        return aligned(px * 128, 128, 128)

    cell = y_lo * NX + x
    plane = []
    column = []
    for d in range(1, 8):
        other = lax.rem(cell + d, 8)
        plane.append((lax.rem(other, NX), lax.div(other, NX)))
        column.append(lax.rem(z + d, NZ))
    arrivals = []
    for d in range(1, 8):
        px, py = plane[d - 1]
        arrivals.append(send(44 + d, msg.at[py, :, strip(px)], recv_a.at[d - 1], device(px, z, py, y_hi, c)))
    summed = msg[y_lo, :, strip(x)].astype(F32)
    for d in range(1, 8):
        arrivals[d - 1].wait_recv()
        summed = summed + recv_a[d - 1].astype(F32)
    summed_b = summed.astype(BF16)
    for b in range(NZ):
        far = (b + 4) % NZ
        stage_b[b, 0:16, :] = summed_b[b * 16 : b * 16 + 16]
        stage_b[b, 16:32, :] = summed_b[far * 16 : far * 16 + 16]
        stage_b[b, 32:48, :] = summed_b[128:144]
    arrivals = []
    for d in (4, 3, 5, 2, 6, 1, 7):
        pz = column[d - 1]
        arrivals.append(send(51 + d, stage_b.at[pz], recv_b.at[d - 1], device(x, pz, y_lo, y_hi, c)))
    for one in arrivals:
        one.wait_recv()
    tile = stage_b[z].astype(F32)
    for d in range(1, 8):
        tile = tile + recv_b[d - 1].astype(F32)
    tile_b = tile.astype(BF16)
    bands = [aligned(z * 16, 16, 16), aligned(lax.rem(z + 4, NZ) * 16, 16, 16)]
    chunk[bands[0], :] = tile_b[0:16]
    chunk[bands[1], :] = tile_b[16:32]
    chunk[128:144, :] = tile_b[32:48]
    arrivals = []
    for n, d in enumerate((6, 1, 7)):
        for m, band in enumerate(bands):
            peer = device(x, column[d - 1], y_lo, y_hi, c)
            arrivals.append(send(59 + 2 * n + m, chunk.at[band], chunk.at[band], peer))
    for one in arrivals:
        one.wait_recv()
    place_mine = table.at[y_hi, c, y_lo, :, strip(x)]
    groups = []
    for dh in range(2):
        for dl in range(2):
            hi = y_hi + dh - 2 * y_hi * dh
            lo = y_lo + dl - 2 * y_lo * dl
            groups.append((dh, dl, hi, lo, []))
    for dx in (2, 1, 3, 0):
        for dh, dl, hi, lo, got in groups[::-1]:
            if dh or dl or dx:
                at = 65 + dh * 8 + dl * 4 + dx
                peer = device(lax.rem(x + dx, NX), z, lo, hi, c)
                got.append(send(at, chunk, place_mine, peer))
    table[y_hi, c, y_lo, :, strip(x)] = chunk[...]
    shared = []
    stores = []

    def store(at, h, core, half):
        row = (h * 2 + core) * 256 + half * 128
        one = pltpu.make_async_copy(table.at[h, core, half, 0:128, :], w_in_out.at[aligned(row, 128, 128), :], out_sem.at[at])
        one.start()
        stores.append(one)

    for n, (dh, dl, hi, lo, got) in enumerate(groups):
        for one in got:
            one.wait_recv()
        part = table.at[hi, c, lo]
        shared.append(send(82 + n, part, part, twin))
        store(n, hi, c, lo)
    for n, (dh, dl, hi, lo, got) in enumerate(groups):
        shared[n].wait_recv()
        store(4 + n, hi, 1 - c, lo)
    b_in_out[...] = table[0, 0, 1, 128:144, :].astype(F32)[0:1]
    for q in range(4):
        w_out_out[q * 16 : q * 16 + 16, :] = table[q // 2, q % 2, 0, 128:144, :].astype(F32)
    for one in started:
        one.wait_send()
    for one in stores:
        one.wait()

    @pl.when(y_hi == 1)
    def _():
        for n in everything:
            share_base(n).wait_send()

    @pl.when(gives_base)
    def _():
        for n in everything:
            to_base(n).wait_send()

    @pl.when(keeps_chain)
    def _():
        for n in everything:
            to_vis(n).wait_send()

    @pl.when(gives_cross)
    def _():
        for n in everything:
            to_cross(n).wait_send()


def write_kernel(feat, w_in, b_in, w_out, feat_out, w_in_out, b_in_out, w_out_out, narrow, wide, load_sem, store_sem):
    count = 4
    rows = [slice(i * DIN // count, (i + 1) * DIN // count) for i in range(count)]
    loads = [pltpu.make_async_copy(w_in.at[r], narrow.at[r], load_sem.at[i]) for i, r in enumerate(rows)]
    stores = [pltpu.make_async_copy(wide.at[r], w_in_out.at[r], store_sem.at[i]) for i, r in enumerate(rows)]
    for one in loads:
        one.start()
    feat_out[...] = feat[...]
    b_in_out[...] = b_in[...]
    w_out_out[...] = w_out[...]
    for i, r in enumerate(rows):
        loads[i].wait()
        wide[r] = narrow[r].astype(F32)
        stores[i].start()
    for one in stores:
        one.wait()


def write(feat, w_in, b_in, w_out):
    free = pl.BlockSpec(memory_space=pltpu.HBM)
    vmem = pl.BlockSpec(memory_space=pltpu.VMEM)
    return pl.pallas_call(
        write_kernel,
        out_shape=tuple(jax.ShapeDtypeStruct(part.shape, F32) for part in (feat, w_in, b_in, w_out)),
        in_specs=[vmem, free, vmem, vmem],
        out_specs=(vmem, free, vmem, vmem),
        scratch_shapes=[
            pltpu.VMEM((DIN, HID), BF16),
            pltpu.VMEM((DIN, HID), F32),
            pltpu.SemaphoreType.DMA((4,)),
            pltpu.SemaphoreType.DMA((4,)),
        ],
        compiler_params=pltpu.CompilerParams(vmem_limit_bytes=56 << 20),
        name="write",
    )(feat, w_in, b_in, w_out)


def on_device(points, w_in, b_in, w_out, inv_scale, solves, probes):
    vmem = pl.BlockSpec(memory_space=pltpu.VMEM)
    hbm = pl.BlockSpec(memory_space=pl.ANY)
    parts = pl.pallas_call(
        kernel,
        out_shape=(
            jax.ShapeDtypeStruct((FEAT, QUARTER), F32),
            jax.ShapeDtypeStruct((DIN, HID), BF16),
            jax.ShapeDtypeStruct((1, HID), F32),
            jax.ShapeDtypeStruct((FEAT, HID), F32),
        ),
        in_specs=[hbm, hbm, vmem, vmem, vmem, hbm, hbm],
        out_specs=(vmem, hbm, vmem, vmem),
        scratch_shapes=[
            pltpu.VMEM((TOK, DIN), BF16),
            pltpu.VMEM((DIN, HID), BF16),
            pltpu.VMEM((TOK, HID), BF16),
            pltpu.VMEM((TOK, HID), F32),
            pltpu.VMEM((256, TOK), BF16),
            pltpu.VMEM((MSG, TOK), BF16),
            pltpu.VMEM((MSG, NX * HALF), BF16),
            pltpu.VMEM((5, MSG, TOK), BF16),
            pltpu.VMEM((3, MSG, TOK), BF16),
            pltpu.VMEM((128, NX * HALF), BF16),
            pltpu.VMEM((AUG, 2 * TOK), BF16),
            pltpu.VMEM((2 * TOK, 128), BF16),
            pltpu.VMEM((2 * TOK, 128), BF16),
            pltpu.VMEM((AUG, NX * HALF), F32),
            pltpu.VMEM((MSG, HALF), BF16),
            pltpu.VMEM((4, FEAT, HALF), BF16),
            pltpu.VMEM((8, FEAT, HALF), BF16),
            pltpu.VMEM((2, FEAT, HALF), BF16),
            pltpu.VMEM((FEAT, TOK), BF16),
            pltpu.VMEM((2, ROWS, HID), BF16),
            pltpu.VMEM((7, ROWS, 128), BF16),
            pltpu.VMEM((NZ, 48, 128), BF16),
            pltpu.VMEM((7, 48, 128), BF16),
            pltpu.VMEM((ROWS, 128), BF16),
            pltpu.VMEM((2, 2, 2, ROWS, HID), BF16),
            pltpu.SemaphoreType.DMA((7,)),
            pltpu.SemaphoreType.DMA((98,)),
            pltpu.SemaphoreType.DMA((98,)),
            pltpu.SemaphoreType.DMA((8,)),
        ],
        compiler_params=pltpu.CompilerParams(
            collective_id=1, has_side_effects=True, vmem_limit_bytes=56 << 20
        ),
        name="trace_term",
    )(points, w_in, b_in[None, :], w_out.T, inv_scale[None, :], solves, probes)
    feat_grad, grad_w_in, grad_b_in, grad_w_out = write(*parts)
    return feat_grad, grad_w_in, grad_b_in[0], grad_w_out.T


def solution(mesh):
    in_specs = (P("blk", None), P(), P(), P(), P(), P(None, "blk"), P(None, "blk"))
    out_specs = (P(None, ("blk", "rep")), P(), P(), P())
    return jax.shard_map(
        on_device, mesh=mesh, in_specs=in_specs, out_specs=out_specs, check_vma=False
    )
```

```python
import math

import jax
import jax.numpy as jnp
from jax import lax
from jax.experimental import pallas as pl
from jax.experimental.pallas import tpu as pltpu
from jax.sharding import PartitionSpec as P

MESH = pl.DeviceIdType.MESH
F32 = jnp.float32
BF16 = jnp.bfloat16
DIN, HID, FEAT, TOK, QUARTER = 1024, 512, 64, 768, 192
HALF = TOK // 2
NX, NZ = 4, 8
ROWS = 144
MSG = 192
AUG = 80
NPTS = 49152


def dot(a, b, ca, cb):
    return lax.dot_general(a, b, (((ca,), (cb,)), ((), ())), preferred_element_type=F32)


def place():
    blk = lax.axis_index("blk")
    rep = lax.axis_index("rep")
    x = lax.rem(blk, NX)
    z = lax.rem(lax.div(blk, NX), NZ)
    y_lo = lax.div(blk, NX * NZ)
    return x, z, y_lo, lax.div(rep, 2), lax.rem(rep, 2)


def device(x, z, y_lo, y_hi, c):
    return ((y_lo * NZ + z) * NX + x, y_hi * 2 + c)


def aligned(start, size, step):
    return pl.ds(pl.multiple_of(start, step), size)


def norm_rows(y, ones_first):
    y32 = y.astype(F32)
    half_sq = -0.5 * jnp.sum(y32 * y32, axis=0, keepdims=True)
    high = half_sq.astype(BF16).astype(F32)
    mid = (half_sq - high).astype(BF16).astype(F32)
    low = (half_sq - high - mid).astype(BF16).astype(F32)
    row = lax.broadcasted_iota(jnp.int32, (16, y.shape[1]), 0)
    base = 3 if ones_first else 0
    ones = 0 if ones_first else 3
    rows = jnp.where((row >= ones) & (row < ones + 3), 1.0, 0.0)
    rows = jnp.where(row == base, high, rows)
    rows = jnp.where(row == base + 1, mid, rows)
    rows = jnp.where(row == base + 2, low, rows)
    return rows.astype(BF16)


def kernel(
    points_in, w_in_any, b_in, w_t, scale_row, solves, probes,
    feat_out, w_in_out, b_in_out, w_out_out,
    points, w_in, hidden, slope, slab_t, own, held, vis, mate, left, vis_b, vis_y, vis_q, acc,
    half_own, part_out, part_in, halves, grad, msg, recv_a, stage_b, recv_b, chunk, table,
    load_sem, send_sem, recv_sem, out_sem,
):
    x, z, y_lo, y_hi, c = place()
    rep = y_hi * 2 + c
    step = 1 - 2 * c
    y_vis = y_lo + y_hi - 2 * y_lo * y_hi
    x_next = lax.rem(x + step + NX, NX)
    x_prev = lax.rem(x - step + NX, NX)
    x_far = lax.rem(x + 2, NX)
    z_next = lax.rem(z + step + NZ, NZ)
    z_prev = lax.rem(z - step + NZ, NZ)
    twin = device(x, z, y_lo, y_hi, 1 - c)
    next_z = device(x, z_next, y_lo, y_hi, c)
    near = [device(one, z, y_lo, y_hi, c) for one in (x_next, x_prev, x_far)]
    near += [device(x, one, y_lo, y_hi, c) for one in (z_next, z_prev)]
    near += [device(x, one, 1 - y_lo, y_hi, c) for one in (z, z_next, z_prev)]
    near += [device(x, one, 1 - y_lo, 1 - y_hi, c) for one in (z, z_next, z_prev)]
    near += [twin, device(x, z, y_lo, 1 - y_hi, c)]

    def lanes(index):
        return aligned(index * HALF, HALF, HALF)

    started = []

    def copy(at, src, dst, peer):
        return pltpu.make_async_remote_copy(
            src_ref=src,
            dst_ref=dst,
            send_sem=send_sem.at[at],
            recv_sem=recv_sem.at[at],
            device_id=peer,
            device_id_type=MESH,
        )

    def send(at, src, dst, peer):
        one = copy(at, src, dst, peer)
        one.start()
        started.append(one)
        return one

    def load(at, src, dst):
        return pltpu.make_async_copy(src, dst, load_sem.at[at])

    barrier = pltpu.get_barrier_semaphore()
    for peer in near:
        pl.semaphore_signal(barrier, inc=1, device_id=peer, device_id_type=MESH)
    loads = []
    for i in range(4):
        part = slice(i * QUARTER, (i + 1) * QUARTER)
        loads.append(load(i, points_in.at[part], points.at[part]))
    loads.insert(0, load(6, w_in_any, w_in))
    loads.append(load(4, solves, own.at[FEAT : 2 * FEAT]))
    loads.append(load(5, probes, own.at[2 * FEAT : MSG]))
    for one in loads:
        one.start()

    def features(i):
        part = slice(i * QUARTER, (i + 1) * QUARTER)
        loads[i + 1].wait()
        pre = dot(points[part], w_in[...], 1, 0) + b_in[...]
        hidden[part] = jnp.tanh(pre).astype(BF16)

    loads[5].wait()
    loads[6].wait()
    pl.semaphore_wait(barrier, len(near))

    pairs = slice(FEAT, MSG)
    feats = slice(0, FEAT)
    pieces = [slice(FEAT, 2 * FEAT), slice(2 * FEAT, MSG), feats]
    vectors = (0, 1)
    everything = (0, 1, 2)
    side = aligned(c * HALF, HALF, HALF)
    x_peers = [device(lax.rem(x + k, NX), z, y_lo, y_hi, c) for k in range(1, 4)]
    visited = device(x, z_next, y_vis, y_hi, c)

    def to_vis(n):
        return copy(n, own.at[pieces[n]], vis.at[1, pieces[n]], visited)

    def to_base(n):
        return copy(3 + n, own.at[pieces[n], side], vis.at[0, pieces[n], side], device(x, z, 1 - y_lo, 1, c))

    def to_cross(n):
        return copy(95 + n, own.at[pieces[n]], vis.at[1, pieces[n]], device(x, z_next, 1 - y_lo, 1, c))

    gives_base = (y_hi + c) == 1
    keeps_chain = (y_hi == 0) | (c == 0)
    gives_cross = (y_hi == 0) & (c == 1)
    takes_cross = (y_hi == 1) & (c == 1)

    def first_sends(which):
        @pl.when(gives_base)
        def _():
            for n in which:
                to_base(n).start()

        @pl.when(keeps_chain)
        def _():
            for n in which:
                to_vis(n).start()

        @pl.when(gives_cross)
        def _():
            for n in which:
                to_cross(n).start()

    def first_arrived(n):
        @pl.when(keeps_chain)
        def _():
            to_vis(n).wait_recv()

        @pl.when(takes_cross)
        def _():
            to_cross(n).wait_recv()

    def share_base(n):
        part = vis.at[0, pieces[n], side]
        return copy(35 + n, part, part, twin)

    def to_z(hop, n):
        at = 6 + 3 * (hop - 1) + n
        if hop < 3:
            return copy(at, vis.at[hop, pieces[n]], vis.at[hop + 1, pieces[n]], next_z)
        return copy(at, vis.at[3, pieces[n], side], vis.at[4, pieces[n], side], next_z)

    def to_mate(hop, n):
        at = 23 + 3 * (hop - 1) + n
        if hop < 4:
            return copy(at, vis.at[hop, pieces[n]], mate.at[hop - 1, pieces[n]], twin)
        part = vis.at[4, pieces[n], side]
        return copy(at, part, part, twin)

    def pump(hop, which):
        for n in which:
            if hop == 1:
                first_arrived(n)
            else:
                to_z(hop - 1, n).wait_recv()
            if hop < 4:
                started.append(to_z(hop, n))
                started[-1].start()
            started.append(to_mate(hop, n))
            started[-1].start()

    def keep_half(rows):
        for q in range(2):
            parts = [own[rows, p * QUARTER : (p + 1) * QUARTER] for p in (2 * q, 2 * q + 1)]
            picked = jnp.where(c == 0, parts[0].astype(F32), parts[1].astype(F32)).astype(BF16)
            half_own[rows, q * QUARTER : (q + 1) * QUARTER] = picked
        held[rows, lanes(x)] = half_own[rows, :]

    first_sends(vectors)
    keep_half(pairs)
    pair_x = {}
    feat_x = {}

    def send_pair(k):
        part = held.at[pairs, lanes(x)]
        pair_x[k] = send(15 + k, part, part, x_peers[k - 1])

    def send_feat(k):
        part = held.at[feats, lanes(x)]
        feat_x[k] = send(19 + k, part, part, x_peers[k - 1])

    send_pair(1)
    send_pair(3)
    send_pair(2)
    loads[0].wait()
    for i in range(4):
        features(i)
    scale_row_v = scale_row[...]
    eye = lax.broadcasted_iota(jnp.int32, (FEAT, FEAT), 0) == lax.broadcasted_iota(jnp.int32, (FEAT, FEAT), 1)
    scale = jnp.sum(jnp.where(eye, scale_row_v, 0.0), axis=1, keepdims=True)
    scaled = (dot(w_t[...], hidden[...], 1, 1) * scale).astype(BF16)
    own[feats, :] = scaled
    first_sends((2,))
    keep_half(feats)
    send_feat(1)
    send_feat(3)
    send_feat(2)

    @pl.when(y_hi == 0)
    def _():
        vis[0] = own[...]

    def ready(index):
        y = held[feats, lanes(index)]
        left[feats, lanes(index)] = y
        left[FEAT:AUG, lanes(index)] = norm_rows(y, False)
        left[AUG:128, lanes(index)] = jnp.zeros((128 - AUG, HALF), BF16)

    def derive(block, at):
        span = slice(at, at + TOK)
        y = block[feats, :]
        augmented = jnp.concatenate([y, norm_rows(y, True)], axis=0)
        vis_b[:, span] = augmented
        padded = jnp.concatenate([augmented, jnp.zeros((128 - AUG, TOK), BF16)], axis=0)
        vis_y[span, :] = padded.T
        swapped = jnp.concatenate([block[2 * FEAT : MSG, :], block[FEAT : 2 * FEAT, :]], axis=0)
        vis_q[span, :] = swapped.T

    def couple(i, at, size):
        span = slice(at, at + size)
        exponent = dot(vis_y[span, :], left[:, i], 1, 0)
        coupling = dot(vis_q[span, :], held[pairs, i], 1, 0)
        weight = (coupling * jnp.exp(exponent)).astype(BF16)
        return dot(vis_b[:, span], weight, 1, 0)

    def meet(k):
        feat_x[k].wait_recv()
        pair_x[k].wait_recv()
        index = lax.rem(x + NX - k, NX)
        ready(index)
        acc[:, lanes(index)] = couple(lanes(index), 0, TOK)

    def visit(block):
        derive(block, 0)
        acc[...] += couple(slice(None), 0, TOK)

    def arrived(hop):
        for n in everything:
            to_mate(hop, n).wait_recv()

    ready(x)

    @pl.when(y_hi == 1)
    def _():
        for n in everything:
            to_base(n).wait_recv()
            share_base(n).start()
        for n in everything:
            share_base(n).wait_recv()

    derive(vis.at[0], 0)
    acc[:, lanes(x)] = couple(lanes(x), 0, TOK)
    slab_t[...] = points[:, aligned(rep * 256, 256, 256)].T
    h32 = hidden[...].astype(F32)
    slope[...] = 1.0 - h32 * h32
    pump(1, vectors)
    meet(1)
    pump(1, (2,))
    meet(3)
    meet(2)
    visit(vis.at[1])
    pump(2, vectors)
    arrived(1)
    visit(mate.at[0])
    pump(2, (2,))
    visit(vis.at[2])
    pump(3, vectors)
    arrived(2)
    visit(mate.at[1])
    pump(3, (2,))
    visit(vis.at[3])
    pump(4, everything)
    arrived(3)
    derive(mate.at[2], 0)
    arrived(4)
    derive(vis.at[4], TOK)

    parts = []

    def finish(k):
        index = lax.rem(x + k, NX)
        i = lanes(index)
        pull = acc[:, i] + couple(i, 0, 2 * TOK)
        drift = pull[feats] - held[feats, i].astype(F32) * pull[FEAT : FEAT + 1]
        part_out[k] = drift.astype(BF16)
        parts.append(send(41 + k, part_out.at[k], part_in.at[4 + k], device(index, z, y_lo, 1 - y_hi, c)))
        if k:
            parts.append(send(37 + k, part_out.at[k], part_in.at[k], device(index, z, y_lo, y_hi, c)))
        return drift

    finish(2)
    finish(1)
    finish(3)
    total = finish(0)
    for one in parts:
        one.wait_recv()
    for k in range(1, 8):
        total = total + part_in[k].astype(F32)
    total = total * scale
    feat_out[...] = jnp.where(y_hi == 0, total[:, 0:QUARTER], total[:, QUARTER:HALF])
    halves[c] = total.astype(BF16)
    send(86, halves.at[c], halves.at[c], twin).wait_recv()
    for q in range(4):
        at = (q // 2) * QUARTER
        grad[:, q * QUARTER : (q + 1) * QUARTER] = halves[q % 2, :, at : at + QUARTER]

    norm = 1.0 / math.sqrt(NPTS)
    pre = dot(grad[...], w_t[...], 0, 0) * slope[...]
    pre_b = pre.astype(BF16)
    def strip(px):
        return aligned(px * 128, 128, 128)

    column = []
    for d in range(1, 8):
        column.append(lax.rem(z + d, NZ))
    arrivals = []

    def scatter(row, first):
        msg[row, 0:128, :] = (dot(slab_t[aligned(row * 128, 128, 128), :], pre_b, 1, 0) * norm).astype(BF16)
        small = jnp.where(row == 0, gwo, bias)
        msg[row, 128:144, :] = small.astype(BF16)
        for dx in (2, 1, 3) if first is None else (2, 1, 3, 0):
            px = lax.rem(x + dx, NX)
            at = (first or 0) + dx
            arrivals.append(send(45 + at, msg.at[row, :, strip(px)], recv_a.at[at], device(px, z, row, y_hi, c)))

    gwo = dot(grad[aligned(rep * 16, 16, 16), :], hidden[...], 1, 0) * norm
    bias = jnp.broadcast_to(jnp.sum(pre, axis=0, keepdims=True) * norm, (16, HID))
    scatter(1 - y_lo, 4)
    scatter(y_lo, None)
    summed = msg[y_lo, :, strip(x)].astype(F32)
    for one in arrivals:
        one.wait_recv()
    for at in range(1, 8):
        summed = summed + recv_a[at].astype(F32)
    summed_b = summed.astype(BF16)
    for b in range(NZ):
        far = (b + 4) % NZ
        stage_b[b, 0:16, :] = summed_b[b * 16 : b * 16 + 16]
        stage_b[b, 16:32, :] = summed_b[far * 16 : far * 16 + 16]
        stage_b[b, 32:48, :] = summed_b[128:144]
    arrivals = []
    for d in (4, 3, 5, 2, 6, 1, 7):
        pz = column[d - 1]
        arrivals.append(send(87 + d, stage_b.at[pz], recv_b.at[d - 1], device(x, pz, y_lo, y_hi, c)))
    for one in arrivals:
        one.wait_recv()
    tile = stage_b[z].astype(F32)
    for d in range(1, 8):
        tile = tile + recv_b[d - 1].astype(F32)
    tile_b = tile.astype(BF16)
    bands = [aligned(z * 16, 16, 16), aligned(lax.rem(z + 4, NZ) * 16, 16, 16)]
    chunk[bands[0], :] = tile_b[0:16]
    chunk[bands[1], :] = tile_b[16:32]
    chunk[128:144, :] = tile_b[32:48]
    arrivals = []
    for n, d in enumerate((6, 1, 7)):
        for m, band in enumerate(bands):
            peer = device(x, column[d - 1], y_lo, y_hi, c)
            arrivals.append(send(59 + 2 * n + m, chunk.at[band], chunk.at[band], peer))
    for one in arrivals:
        one.wait_recv()
    place_mine = table.at[y_hi, c, y_lo, :, strip(x)]
    groups = []
    for dh in range(2):
        for dl in range(2):
            hi = y_hi + dh - 2 * y_hi * dh
            lo = y_lo + dl - 2 * y_lo * dl
            groups.append((dh, dl, hi, lo, []))
    for dx in (2, 1, 3, 0):
        for dh, dl, hi, lo, got in groups[::-1]:
            if dh or dl or dx:
                at = 65 + dh * 8 + dl * 4 + dx
                peer = device(lax.rem(x + dx, NX), z, lo, hi, c)
                got.append(send(at, chunk, place_mine, peer))
    table[y_hi, c, y_lo, :, strip(x)] = chunk[...]
    shared = []
    stores = []

    def store(at, h, core, half):
        row = (h * 2 + core) * 256 + half * 128
        one = pltpu.make_async_copy(table.at[h, core, half, 0:128, :], w_in_out.at[aligned(row, 128, 128), :], out_sem.at[at])
        one.start()
        stores.append(one)

    for n, (dh, dl, hi, lo, got) in enumerate(groups):
        for one in got:
            one.wait_recv()
        part = table.at[hi, c, lo]
        shared.append(send(82 + n, part, part, twin))
        store(n, hi, c, lo)
    for n, (dh, dl, hi, lo, got) in enumerate(groups):
        shared[n].wait_recv()
        store(4 + n, hi, 1 - c, lo)
    b_in_out[...] = table[0, 0, 1, 128:144, :].astype(F32)[0:1]
    for q in range(4):
        w_out_out[q * 16 : q * 16 + 16, :] = table[q // 2, q % 2, 0, 128:144, :].astype(F32)
    for one in started:
        one.wait_send()
    for one in stores:
        one.wait()

    @pl.when(y_hi == 1)
    def _():
        for n in everything:
            share_base(n).wait_send()

    @pl.when(gives_base)
    def _():
        for n in everything:
            to_base(n).wait_send()

    @pl.when(keeps_chain)
    def _():
        for n in everything:
            to_vis(n).wait_send()

    @pl.when(gives_cross)
    def _():
        for n in everything:
            to_cross(n).wait_send()


def write_kernel(feat, w_in, b_in, w_out, feat_out, w_in_out, b_in_out, w_out_out, narrow, wide, load_sem, store_sem):
    count = 4
    rows = [slice(i * DIN // count, (i + 1) * DIN // count) for i in range(count)]
    loads = [pltpu.make_async_copy(w_in.at[r], narrow.at[r], load_sem.at[i]) for i, r in enumerate(rows)]
    stores = [pltpu.make_async_copy(wide.at[r], w_in_out.at[r], store_sem.at[i]) for i, r in enumerate(rows)]
    for one in loads:
        one.start()
    feat_out[...] = feat[...]
    b_in_out[...] = b_in[...]
    w_out_out[...] = w_out[...]
    for i, r in enumerate(rows):
        loads[i].wait()
        wide[r] = narrow[r].astype(F32)
        stores[i].start()
    for one in stores:
        one.wait()


def write(feat, w_in, b_in, w_out):
    free = pl.BlockSpec(memory_space=pltpu.HBM)
    vmem = pl.BlockSpec(memory_space=pltpu.VMEM)
    return pl.pallas_call(
        write_kernel,
        out_shape=tuple(jax.ShapeDtypeStruct(part.shape, F32) for part in (feat, w_in, b_in, w_out)),
        in_specs=[vmem, free, vmem, vmem],
        out_specs=(vmem, free, vmem, vmem),
        scratch_shapes=[
            pltpu.VMEM((DIN, HID), BF16),
            pltpu.VMEM((DIN, HID), F32),
            pltpu.SemaphoreType.DMA((4,)),
            pltpu.SemaphoreType.DMA((4,)),
        ],
        compiler_params=pltpu.CompilerParams(vmem_limit_bytes=56 << 20),
        name="write",
    )(feat, w_in, b_in, w_out)


def on_device(points, w_in, b_in, w_out, inv_scale, solves, probes):
    vmem = pl.BlockSpec(memory_space=pltpu.VMEM)
    hbm = pl.BlockSpec(memory_space=pl.ANY)
    parts = pl.pallas_call(
        kernel,
        out_shape=(
            jax.ShapeDtypeStruct((FEAT, QUARTER), F32),
            jax.ShapeDtypeStruct((DIN, HID), BF16),
            jax.ShapeDtypeStruct((1, HID), F32),
            jax.ShapeDtypeStruct((FEAT, HID), F32),
        ),
        in_specs=[hbm, hbm, vmem, vmem, vmem, hbm, hbm],
        out_specs=(vmem, hbm, vmem, vmem),
        scratch_shapes=[
            pltpu.VMEM((TOK, DIN), BF16),
            pltpu.VMEM((DIN, HID), BF16),
            pltpu.VMEM((TOK, HID), BF16),
            pltpu.VMEM((TOK, HID), F32),
            pltpu.VMEM((256, TOK), BF16),
            pltpu.VMEM((MSG, TOK), BF16),
            pltpu.VMEM((MSG, NX * HALF), BF16),
            pltpu.VMEM((5, MSG, TOK), BF16),
            pltpu.VMEM((3, MSG, TOK), BF16),
            pltpu.VMEM((128, NX * HALF), BF16),
            pltpu.VMEM((AUG, 2 * TOK), BF16),
            pltpu.VMEM((2 * TOK, 128), BF16),
            pltpu.VMEM((2 * TOK, 128), BF16),
            pltpu.VMEM((AUG, NX * HALF), F32),
            pltpu.VMEM((MSG, HALF), BF16),
            pltpu.VMEM((4, FEAT, HALF), BF16),
            pltpu.VMEM((8, FEAT, HALF), BF16),
            pltpu.VMEM((2, FEAT, HALF), BF16),
            pltpu.VMEM((FEAT, TOK), BF16),
            pltpu.VMEM((2, ROWS, HID), BF16),
            pltpu.VMEM((8, ROWS, 128), BF16),
            pltpu.VMEM((NZ, 48, 128), BF16),
            pltpu.VMEM((7, 48, 128), BF16),
            pltpu.VMEM((ROWS, 128), BF16),
            pltpu.VMEM((2, 2, 2, ROWS, HID), BF16),
            pltpu.SemaphoreType.DMA((7,)),
            pltpu.SemaphoreType.DMA((98,)),
            pltpu.SemaphoreType.DMA((98,)),
            pltpu.SemaphoreType.DMA((8,)),
        ],
        compiler_params=pltpu.CompilerParams(
            collective_id=1, has_side_effects=True, vmem_limit_bytes=56 << 20
        ),
        name="trace_term",
    )(points, w_in, b_in[None, :], w_out.T, inv_scale[None, :], solves, probes)
    feat_grad, grad_w_in, grad_b_in, grad_w_out = write(*parts)
    return feat_grad, grad_w_in, grad_b_in[0], grad_w_out.T


def solution(mesh):
    in_specs = (P("blk", None), P(), P(), P(), P(), P(None, "blk"), P(None, "blk"))
    out_specs = (P(None, ("blk", "rep")), P(), P(), P())
    return jax.shard_map(
        on_device, mesh=mesh, in_specs=in_specs, out_specs=out_specs, check_vma=False
    )
```
